32 devices in a mesh: ctx: 8 (over y, x, core), head: 4 (over z).
Axes of the slice: x: 2, y: 2, z: 4, core: 2. Of those that a mesh axis runs over, the one named last changes fastest.
Arguments:
- head_inputs: bfloat16 [8192, 8192], P(('ctx', 'head')), may hold values from -6 to 6
- gate_inputs: bfloat16 [8192, 8192], P(('ctx', 'head')), may hold values from -6 to 6
- write_keys: bfloat16 [8192, 1024], P(('ctx', 'head')), may hold values from -6 to 6
- read_queries: bfloat16 [8192, 1024], P(('ctx', 'head')), may hold values from -0.5 to 0.5
- step_logits: bfloat16 [8192, 128], P(('ctx', 'head')), may hold values from -3 to 3
- step_bias: float32 [128], P('head'), may hold values from -6 to 0
- decay_log: float32 [128], P('head'), may hold values from -7 to -2
- skip_scale: float32 [128], P('head'), may hold values from 0.5 to 1.5
- norm_gain: float32 [8192], replicated, may hold values from 0.1 to 1.9
- document_starts: int32 [32], P('ctx'), may hold values from 0 to 256, as said below
Outputs:
- layer_output: bfloat16 [8192, 8192], P(('ctx', 'head'))
The draws below stay inside these ranges and needn't reach their ends.
Inputs may be any that keep to these rules, and one draw needn't show every extreme that they name: `document_starts`: each entry is the position within its block of 256 tokens at which a document starts, or 256 where none starts; the first block starts one at 0.
All inputs are finite; a program needn't handle non-finite values.
Results may differ from the reference program's by a relative error of at most 0.0058.
Values may be sent and summed in bfloat16 or wider, within the bound.
A program may use at most 128 MiB of HBM per device.

```python
import jax
import jax.numpy as jnp
from jax import lax

HEADS = 128
HEAD_DIM = 64
STATE = 128
GROUPS = 8
BLOCK = 256
INNER = 8192
TOKENS = 8192


def decay_heads(key):
    rand_key = jax.random.fold_in(key, 11)
    spread = jax.random.uniform(rand_key, (HEADS,), jnp.float32)
    memory = 30.0 * (TOKENS / 30.0) ** spread
    step_size = 2.0 / jnp.sqrt(memory)
    return (memory, step_size)


def draw_step_bias(key, part):
    memory, step_size = decay_heads(key)
    return jnp.log(jnp.expm1(step_size)).astype(jnp.float32)


def draw_decay_log(key, part):
    memory, step_size = decay_heads(key)
    return (-jnp.log(memory * step_size)).astype(jnp.float32)


def draw_document_starts(key, part):
    count = TOKENS // BLOCK
    spacing = max(count // 4, 2)
    raw_draw = jax.random.randint(jax.random.fold_in(key, 5), (count,), 0, spacing * BLOCK)
    starts = jnp.where(raw_draw < BLOCK, raw_draw, BLOCK)
    return starts.at[0].set(0).astype(jnp.int32)


def steps_of(key, extent, pieces, smallest, largest):
    factor_of, own = 1.0, jax.random.fold_in(key, 6)
    for dim, shards_of in pieces:
        draws = jnp.exp(jax.random.uniform(jax.random.fold_in(own, dim), (shards_of,), jnp.float32, smallest / len(pieces), largest / len(pieces)))
        factor_of = factor_of * jnp.repeat(draws, extent[dim] // shards_of).reshape([-1 if axis == dim else 1 for axis in range(len(extent))])
    return factor_of


def gaussian(key, extent, width, most, pieces=(), kind=jnp.bfloat16):
    drawn = width * jax.random.normal(key, extent, jnp.float32)
    if pieces:
        drawn = drawn * steps_of(key, extent, pieces, -0.22, 0.18)
    return jnp.clip(drawn, -most, most).astype(kind)


def setup_inputs(seed: int = 0) -> dict:
    seeds = jax.random.split(jax.random.key(seed), 11)
    return {
        "head_inputs": gaussian(seeds[0], (TOKENS, INNER), 1.0, 6.0, ((0, 32),)),
        "gate_inputs": gaussian(seeds[1], (TOKENS, INNER), 1.0, 6.0, ((0, 32),)),
        "write_keys": gaussian(seeds[2], (TOKENS, GROUPS * STATE), 1.0, 6.0, ((0, 32),)),
        "read_queries": gaussian(seeds[3], (TOKENS, GROUPS * STATE), STATE ** -0.5, 0.5, ((0, 32),)),
        "step_logits": gaussian(seeds[4], (TOKENS, HEADS), 0.5, 3.0, ((0, 32),)),
        "step_bias": draw_step_bias(jax.random.fold_in(seeds[10], 71), 0),
        "decay_log": draw_decay_log(jax.random.fold_in(seeds[10], 71), 0),
        "skip_scale": jnp.clip(0.5 + 1.0 * jax.random.uniform(seeds[7], (HEADS,), jnp.float32) ** steps_of(seeds[7], (HEADS,), ((0, 4),), -0.2, 0.2), 0.5, 1.5),
        "norm_gain": jnp.clip(1.0 + 0.18 * jax.random.normal(seeds[8], (INNER,), jnp.float32), 0.1, 1.9),
        "document_starts": draw_document_starts(jax.random.fold_in(seeds[10], 71), 0),
    }


def block_terms(block_x, block_b, block_c, block_logit, start_at, step_bias, decay_log):
    length = block_x.shape[0]
    per_group = block_x.shape[1] // block_b.shape[1]
    step_size = jax.nn.softplus(block_logit.astype(jnp.float32) + step_bias)
    log_decay = -jnp.exp(decay_log) * step_size
    cumulative = jnp.cumsum(log_decay, axis=0)
    position = jnp.arange(length, dtype=jnp.int32)
    segment = position >= start_at
    allowed = (segment[:, None] == segment[None, :]) & (position[:, None] >= position[None, :])
    scores = jnp.einsum('tgn,sgn->gts', block_c.astype(jnp.float32), block_b.astype(jnp.float32))
    scores = jnp.repeat(scores, per_group, axis=0)
    across = cumulative.T
    spread = across[:, :, None] - across[:, None, :]
    damping = jnp.where(allowed[None], jnp.exp(jnp.where(allowed[None], spread, 0.0)), 0.0)
    mixing = lax.optimization_barrier((damping * scores * step_size.T[:, None, :]).astype(jnp.bfloat16))
    inside = jnp.einsum('hts,shp->thp', mixing.astype(jnp.float32), block_x.astype(jnp.float32))
    keep = segment == segment[length - 1]
    tail = jnp.where(keep[:, None], jnp.exp(cumulative[length - 1][None, :] - cumulative), 0.0) * step_size
    scaled = lax.optimization_barrier((block_x.astype(jnp.float32) * tail[:, :, None]).astype(jnp.bfloat16))
    keys_heads = jnp.repeat(block_b, per_group, axis=1)
    written = jnp.einsum('thp,thn->hpn', scaled.astype(jnp.float32), keys_heads.astype(jnp.float32))
    carried = jnp.where(start_at >= length, jnp.exp(cumulative[length - 1]), 0.0)
    return (inside, written, carried, cumulative, segment)

def reference(head_inputs, gate_inputs, write_keys, read_queries, step_logits, step_bias, decay_log, skip_scale, norm_gain, document_starts):
    blocks = TOKENS // BLOCK
    per_group = HEADS // GROUPS
    x_blocks = head_inputs.reshape(blocks, BLOCK, HEADS, HEAD_DIM)
    b_blocks = write_keys.reshape(blocks, BLOCK, GROUPS, STATE)
    c_blocks = read_queries.reshape(blocks, BLOCK, GROUPS, STATE)
    logit_blocks = step_logits.reshape(blocks, BLOCK, HEADS)

    def advance(carry_state, items):
        block_x, block_b, block_c, block_logit, start_at = items
        inside, written, carried, cumulative, segment = block_terms(block_x, block_b, block_c, block_logit, start_at, step_bias, decay_log)
        frozen = lax.optimization_barrier(carry_state.astype(jnp.bfloat16))
        query_heads = jnp.repeat(block_c, per_group, axis=1)
        outside = jnp.einsum('thn,hpn->thp', query_heads.astype(jnp.float32), frozen.astype(jnp.float32))
        factor = jnp.where(segment[:, None], 0.0, jnp.exp(cumulative))
        mixed = (inside + outside * factor[:, :, None] + skip_scale[None, :, None] * block_x.astype(jnp.float32)).astype(jnp.bfloat16)
        next_state = carried[:, None, None] * carry_state + written
        return (next_state, mixed)
    initial = jnp.zeros((HEADS, HEAD_DIM, STATE), jnp.float32)
    _, mixed = lax.scan(advance, initial, (x_blocks, b_blocks, c_blocks, logit_blocks, document_starts))
    scanned = mixed.reshape(TOKENS, HEADS * HEAD_DIM)
    gated = scanned.astype(jnp.float32) * jax.nn.silu(gate_inputs.astype(jnp.float32))
    power = lax.optimization_barrier(jnp.mean(gated * gated, axis=-1, keepdims=True))
    return (gated * lax.rsqrt(power + 1e-05) * norm_gain).astype(jnp.bfloat16)
```

```python
import functools

import jax
import jax.numpy as jnp
from jax import lax
from jax.experimental import pallas as pl
from jax.experimental.pallas import tpu as pltpu
from jax.sharding import PartitionSpec as P

HEAD_DIM = 64
STATE = 128
BLOCK = 256
CHUNK = 256
SKEW = 3
TURN = 3
ROWS = 32
MESH = pl.DeviceIdType.MESH
F32 = jnp.float32
BF16 = jnp.bfloat16


def split_terms(value, terms):
    parts = []
    for _ in range(terms):
        part = value.astype(BF16)
        parts.append(part)
        value = value - part.astype(F32)
    return parts


def widen(table, ref):
    lane = lax.broadcasted_iota(jnp.int32, (table.shape[0], 128), 1)
    per_tile = 128 // HEAD_DIM
    for j in range(ref.shape[1] // 128):
        tile = jnp.broadcast_to(table[:, j * per_tile : j * per_tile + 1], lane.shape)
        for i in range(1, per_tile):
            column = j * per_tile + i
            tile = jnp.where(lane >= i * HEAD_DIM, jnp.broadcast_to(table[:, column : column + 1], lane.shape), tile)
        ref[:, j * 128 : (j + 1) * 128] = tile


def exchange_kernel(
    n, m, groups,
    x_hbm, gate_hbm, b_hbm, c_hbm, logit_hbm, bias_hbm, decay_hbm, skip_hbm, starts_hbm,
    gated_ref, power_ref,
    x_ref, gate_ref, b_ref, c_ref, logit_ref, bias_ref, decay_ref, skip_ref, starts_ref,
    keys_ref, scores_ref, spread_ref, param_ref,
    tail_ref, up_ref, down_ref, out_ref, skips_ref, line_ref, coef_ref,
    own_ref, sum_ref, before_ref, inside_ref,
    step_send, step_recv, fore_send, fore_recv, back_send, back_recv,
    param_in, decay_out, decay_in, hop_out, hop_in,
    param_sems, decay_sems, hop_sems, step_sems, fore_sems, back_sems, load_sems,
):
    ci = lax.axis_index("ctx")
    zi = lax.axis_index("head")
    bits = m.bit_length() - 1
    length, inner = x_ref.shape
    heads = logit_ref.shape[1]
    count = inner // CHUNK
    per_group = count // groups
    chunk_heads = CHUNK // HEAD_DIM

    half = count // max(n, 4)
    first = 2 * half
    second = count - first
    z_turn = max(first, TURN + bits * SKEW)
    c_turn = max(TURN + second, (n - 1) * SKEW)

    def first_chunk(i):
        return jnp.where(i < half, i, count - first + i)

    def second_chunk(i):
        return half + i

    pairs = (
        (bias_hbm, bias_ref), (decay_hbm, decay_ref), (skip_hbm, skip_ref), (starts_hbm, starts_ref),
        (b_hbm, b_ref), (c_hbm, c_ref), (logit_hbm, logit_ref), (x_hbm, x_ref), (gate_hbm, gate_ref),
    )
    loads = [pltpu.make_async_copy(src, dst, load_sems.at[i]) for i, (src, dst) in enumerate(pairs)]
    for load in loads:
        load.start()

    def z_peer(d):
        return (ci, lax.rem(zi + d, n))

    def ctx_peer(d):
        return (lax.rem(ci + d, m), zi)

    def ctx_partner(j):
        bit = 1 << j
        upper = lax.rem(ci // bit, 2)
        return ci + bit - 2 * bit * upper, upper

    barrier = pltpu.get_barrier_semaphore()
    for d in range(1, n):
        pl.semaphore_signal(barrier, inc=1, device_id=z_peer(d), device_id_type=MESH)
    for d in range(1, m):
        pl.semaphore_signal(barrier, inc=1, device_id=ctx_peer(d), device_id_type=MESH)

    own_heads = bias_ref.shape[1]
    place = jnp.where(
        lax.broadcasted_iota(jnp.int32, (own_heads, heads), 0) + zi * own_heads
        == lax.broadcasted_iota(jnp.int32, (own_heads, heads), 1), 1.0, 0.0
    ).astype(BF16)
    for load in loads[:4]:
        load.wait()
    raw = jnp.concatenate(
        [bias_ref[...], decay_ref[...], skip_ref[...], jnp.zeros((5, own_heads), F32)], axis=0
    )
    placed = jnp.zeros((8, heads), F32)
    for part in split_terms(raw, 3):
        placed = placed + jnp.dot(part, place, preferred_element_type=F32)
    param_ref[...] = placed

    def remote(src, dst, sems, index, device):
        return pltpu.make_async_remote_copy(
            src_ref=src, dst_ref=dst, send_sem=sems.at[(0, *index)], recv_sem=sems.at[(1, *index)],
            device_id=device, device_id_type=MESH,
        )

    param_copies = [
        remote(param_ref, param_in.at[d], param_sems, (d,), z_peer(d)) for d in range(1, n)
    ]
    decay_copies = [
        remote(decay_out, decay_in.at[d], decay_sems, (d,), z_peer(d)) for d in range(1, n)
    ]
    hop_copies = [
        remote(hop_out, hop_in.at[d], hop_sems, (d,), ctx_peer(d)) for d in range(1, m)
    ]
    pl.semaphore_wait(barrier, n - 1 + m - 1)
    for copy in param_copies:
        copy.start()

    row = lax.broadcasted_iota(jnp.int32, (2 * heads, CHUNK), 0)
    lane = lax.broadcasted_iota(jnp.int32, (2 * heads, CHUNK), 1)

    def fill(k, _):
        own = lane // HEAD_DIM + k * chunk_heads
        spread_ref[k] = jnp.where((row == own) | (row == own + heads), 1.0, 0.0).astype(BF16)
        return 0

    lax.fori_loop(0, count, fill, 0)

    offset = lax.rem(zi * length, BLOCK)
    starts = starts_ref[...].astype(F32)
    mine = lax.broadcasted_iota(jnp.int32, starts.shape, 1) == zi * length // BLOCK
    start = jnp.sum(jnp.where(mine, starts, 0.0), axis=1, keepdims=True) - offset.astype(F32)
    start = jnp.where((start < 0.0) | (start >= length), float(length), start)
    row = lax.broadcasted_iota(jnp.int32, (length, length), 0).astype(F32)
    col = lax.broadcasted_iota(jnp.int32, (length, length), 1).astype(F32)
    lower = jnp.where(row >= col, 1.0, 0.0)
    same = jnp.where(row >= start, 1.0, 0.0) == jnp.where(col >= start, 1.0, 0.0)
    allowed = jnp.where(same, lower, 0.0)
    for load in loads[4:7]:
        load.wait()
    for g in range(groups):
        part = slice(g * STATE, (g + 1) * STATE)
        scores = lax.dot_general(
            c_ref[:, part], b_ref[:, part], (((1,), (1,)), ((), ())), preferred_element_type=F32
        )
        scores_ref[g] = jnp.where(allowed > 0.0, scores, 0.0).astype(BF16)
        keys_ref[g] = b_ref[:, part].astype(F32).T.astype(BF16)
    power_ref[...] = jnp.zeros_like(power_ref)

    for copy in param_copies:
        copy.wait()
    params = param_ref[...]
    for d in range(1, n):
        params = params + param_in[d]

    logits = logit_ref[...].astype(F32) + params[0:1]
    step = jnp.maximum(logits, 0.0) + jnp.log1p(jnp.exp(-jnp.abs(logits)))
    rate = -jnp.exp(params[1:2]) * step
    lower = lower.astype(BF16)
    cum = jnp.zeros((length, heads), F32)
    for part in split_terms(rate, 3)[::-1]:
        cum = cum + jnp.dot(lower, part, preferred_element_type=F32)
    last = cum[length - 1 : length]
    middle = cum[length // 2 - 1 : length // 2]
    position = lax.broadcasted_iota(jnp.int32, (length, heads), 0).astype(F32)
    begins = start < length
    carried = jnp.where(begins, 0.0, jnp.exp(last))

    decay_out[...] = jnp.broadcast_to(carried, decay_out.shape)
    for copy in decay_copies:
        copy.start()
    keep = position >= jnp.where(begins, start, 0.0)
    tail = jnp.where(keep, jnp.exp(last - cum), 0.0) * step
    tail_ref[...] = jnp.concatenate(split_terms(tail, 2), axis=1)
    up_ref[...] = jnp.concatenate(split_terms(jnp.exp(cum - middle), 2), axis=1)
    down_ref[...] = jnp.concatenate(split_terms(jnp.exp(middle - cum) * step, 2), axis=1)
    out_ref[...] = jnp.concatenate(
        split_terms(jnp.where(position < start, jnp.exp(cum), 0.0), 2), axis=1
    )
    widen(jnp.broadcast_to(params[2:3], (8, heads)), skips_ref)
    loads[7].wait()
    loads[8].wait()

    def step_copy(j, k):
        return remote(step_send.at[j, k], step_recv.at[j, k], step_sems, (j, k), (ctx_partner(j)[0], zi))

    def fore_copy(k):
        return remote(fore_send.at[k], fore_recv.at[k], fore_sems, (k,), (ci, lax.rem(zi + 1, n)))

    def back_copy(k):
        return remote(back_send.at[k], back_recv.at[k], back_sems, (k,), (ci, lax.rem(zi + n - 1, n)))

    def channels(k):
        return pl.ds(pl.multiple_of(k * CHUNK, CHUNK), CHUNK)

    def states(k):
        return pl.ds(pl.multiple_of((k // per_group) * STATE, STATE), STATE)

    def line(k, slot):
        return line_ref[slot : slot + 1, channels(k)]

    def coef(k, slot):
        return coef_ref[slot : slot + 1, channels(k)]

    is_last_upper = ctx_partner(bits - 1)[1] == 1
    is_last_lower = ctx_partner(bits - 1)[1] == 0

    def write(k):
        weight = jnp.dot(tail_ref[...], spread_ref[k], preferred_element_type=F32)
        scaled = (x_ref[:, channels(k)].astype(F32) * weight).astype(BF16)
        written = jnp.dot(keys_ref[k // per_group], scaled, preferred_element_type=F32)
        own_ref[k] = written
        return written

    def enter(k, value):
        sum_ref[k] = value
        step_send[0, k] = value.astype(BF16)
        step_copy(0, k).start()

    def look(k):
        x = x_ref[:, channels(k)].astype(F32)
        down = jnp.dot(down_ref[...], spread_ref[k], preferred_element_type=F32)
        up = jnp.dot(up_ref[...], spread_ref[k], preferred_element_type=F32)
        inside = jnp.dot(scores_ref[k // per_group], (x * down).astype(BF16), preferred_element_type=F32)
        inside_ref[k] = up * inside + skips_ref[0:1, channels(k)] * x

    def finish(k, with_back):
        incoming = before_ref[k]
        if with_back:
            incoming = incoming + back_recv[k].astype(F32)
        frozen = (fore_recv[k].astype(F32) + line(k, 1) * incoming).astype(BF16)
        outside = jnp.dot(c_ref[:, states(k)], frozen, preferred_element_type=F32)
        weight = jnp.dot(out_ref[...], spread_ref[k], preferred_element_type=F32)
        gate = gate_ref[:, channels(k)].astype(F32)
        gated = (outside * weight + inside_ref[k]) * (gate / (1.0 + jnp.exp(-gate)))
        gated_ref[:, channels(k)] = gated.astype(BF16)
        square = gated * gated
        total = power_ref[...]
        for i in range(CHUNK // 128):
            total = total + square[:, i * 128 : (i + 1) * 128]
        power_ref[...] = total

    fore_at = zi * SKEW
    back_at = (n - 1 - zi) * SKEW
    done_at = jnp.maximum(fore_at, back_at)

    def iteration(t, _):
        @pl.when(t == TURN)
        def _():
            for copy in decay_copies:
                copy.wait()
            own = decay_out[...]
            before = jnp.ones((8, heads), F32)
            after = jnp.ones((8, heads), F32)
            for d in range(1, n):
                got = decay_in[d]
                before = before * jnp.where(zi >= d, got, 1.0)
                after = after * jnp.where(zi >= d, 1.0, got)
            hop_out[...] = before * own * after
            for copy in hop_copies:
                copy.start()
            widen(jnp.concatenate([own[0:1], before[0:1], after[0:1], own[3:8]], axis=0), line_ref)

        @pl.when(t == TURN + SKEW)
        def _():
            for copy in hop_copies:
                copy.wait()
            total = hop_out[...]
            ahead = jnp.ones((8, heads), F32)
            rows = []
            for j in range(bits):
                bit = 1 << j
                is_upper = ctx_partner(j)[1] == 1
                sibling = ctx_partner(j)[0] // bit
                got = jnp.ones((8, heads), F32)
                for d in range(1, m):
                    source = lax.rem(ci + m - d, m)
                    got = got * jnp.where(source // bit == sibling, hop_in[d], 1.0)
                rows.append(jnp.where(is_upper, 1.0, got))
                rows.append(jnp.where(is_upper, total, 1.0))
                rows.append(jnp.where(is_upper, ahead, 0.0))
                ahead = jnp.where(is_upper, ahead * got, ahead)
                total = total * got
            pad = [jnp.zeros((1, heads), F32)] * (coef_ref.shape[0] - len(rows))
            widen(jnp.concatenate([r[0:1] for r in rows] + pad, axis=0), coef_ref)

        @pl.when(t < first)
        def _():
            write(first_chunk(t))


        def fore(k, is_first):
            @pl.when(zi > 0)
            def _():
                fore_copy(k).wait_recv()

            @pl.when(zi == 0)
            def _():
                fore_recv[k] = jnp.zeros_like(fore_recv[k])
                if is_first:
                    fore_send[k] = own_ref[k].astype(BF16)
                    fore_copy(k).start()

            @pl.when((zi > 0) & (zi < n - 1) if is_first else zi < n - 1)
            def _():
                arrived = fore_recv[k].astype(F32)
                if not is_first:
                    arrived = arrived + line(k, 1) * before_ref[k]
                fore_send[k] = (line(k, 0) * arrived + own_ref[k]).astype(BF16)
                fore_copy(k).start()

        def back(k, is_first):
            @pl.when(zi < n - 1)
            def _():
                back_copy(k).wait_recv()

            @pl.when(zi == n - 1)
            def _():
                back_recv[k] = jnp.zeros_like(back_recv[k])
                if is_first:
                    back_send[k] = own_ref[k].astype(BF16)
                    back_copy(k).start()

            @pl.when((zi > 0) & (zi < n - 1) if is_first else zi > 0)
            def _():
                more = line(k, 2) * own_ref[k] if is_first else before_ref[k]
                back_send[k] = (back_recv[k].astype(F32) + more).astype(BF16)
                back_copy(k).start()

        for at, relay in ((fore_at, fore), (back_at, back)):
            s = t - at

            @pl.when((s >= 0) & (s < first))
            def _():
                relay(first_chunk(s), True)

            @pl.when((s >= z_turn) & (s < z_turn + second))
            def _():
                relay(second_chunk(s - z_turn), False)

        for j in range(bits):
            s = t - (j + 1) * SKEW
            is_second = (s >= TURN) & (s < TURN + second)
            is_first = (s >= c_turn) & (s < c_turn + first)

            @pl.when(is_second | is_first)
            def _(j=j, s=s):
                k = jnp.where(s < TURN + second, second_chunk(s - TURN), first_chunk(s - c_turn))

                def receive():
                    step_copy(j, k).wait_recv()
                    got = step_recv[j, k].astype(F32)
                    part = coef(k, 2 + 3 * j) * got
                    before_ref[k] = part if j == 0 else before_ref[k] + part
                    return got

                if j == bits - 1:
                    @pl.when(is_last_upper)
                    def _():
                        receive()

                else:
                    got = receive()
                    value = sum_ref[k] * coef(k, 3 * j) + coef(k, 1 + 3 * j) * got
                    sum_ref[k] = value

                    def send():
                        step_send[j + 1, k] = value.astype(BF16)
                        step_copy(j + 1, k).start()

                    if j == bits - 2:
                        pl.when(is_last_lower)(send)
                    else:
                        send()

        @pl.when((t >= TURN) & (t < TURN + second))
        def _():
            k = second_chunk(t - TURN)
            enter(k, line(k, 2) * write(k))

        @pl.when((t >= c_turn) & (t < c_turn + first))
        def _():
            k = first_chunk(t - c_turn)
            value = line(k, 0) * fore_recv[k].astype(F32) + own_ref[k]
            enter(k, line(k, 2) * value + back_recv[k].astype(F32))

        s = t - z_turn - done_at

        @pl.when((s >= 0) & (s < second))
        def _():
            finish(second_chunk(s), True)

        r = t - c_turn - bits * SKEW

        @pl.when((r >= 0) & (r < first))
        def _():
            finish(first_chunk(r), False)

        @pl.when(t < count)
        def _():
            look(t)

        return 0

    steps = max(z_turn + second + (n - 1) * SKEW, c_turn + first + bits * SKEW)
    lax.fori_loop(0, steps, iteration, 0)

    def drain(k, _):
        for j in range(bits - 1):
            step_copy(j, k).wait_send()

        @pl.when(is_last_lower)
        def _():
            step_copy(bits - 1, k).wait_send()

        @pl.when(zi < n - 1)
        def _():
            fore_copy(k).wait_send()

        @pl.when(zi > 0)
        def _():
            back_copy(k).wait_send()

        return 0

    lax.fori_loop(0, count, drain, 0)


def scale_kernel(gated_ref, power_ref, gain_ref, out_ref):
    inner = gated_ref.shape[1]
    power = jnp.sum(power_ref[...], axis=1, keepdims=True)
    factor = lax.rsqrt(power / inner + 1e-05)
    width = 1024
    for i in range(inner // width):
        part = slice(i * width, (i + 1) * width)
        out_ref[:, part] = (gated_ref[:, part].astype(F32) * factor * gain_ref[:, part]).astype(BF16)


def local(
    n, m,
    head_inputs, gate_inputs, write_keys, read_queries, step_logits,
    step_bias, decay_log, skip_scale, norm_gain, document_starts,
):
    length, inner = head_inputs.shape
    heads = step_logits.shape[1]
    groups = write_keys.shape[1] // STATE
    assert length <= BLOCK and BLOCK % length == 0 and m & (m - 1) == 0 and m > 2 and n > 1
    bits = m.bit_length() - 1
    count = inner // CHUNK
    coefs = -(-3 * bits // 8) * 8
    assert TURN <= SKEW and count % max(n, 4) == 0

    hbm = pl.BlockSpec(memory_space=pltpu.HBM)
    whole = pl.BlockSpec(memory_space=pltpu.VMEM)
    piece = (count, STATE, CHUNK)
    dma = pltpu.SemaphoreType.DMA
    gated, power = pl.pallas_call(
        functools.partial(exchange_kernel, n, m, groups),
        out_shape=(
            jax.ShapeDtypeStruct((length, inner), BF16),
            jax.ShapeDtypeStruct((length, 128), F32),
        ),
        in_specs=[hbm] * 9,
        out_specs=(whole, whole),
        scratch_shapes=[
            pltpu.VMEM((length, inner), BF16),
            pltpu.VMEM((length, inner), BF16),
            pltpu.VMEM(write_keys.shape, BF16),
            pltpu.VMEM(read_queries.shape, BF16),
            pltpu.VMEM(step_logits.shape, BF16),
            pltpu.VMEM((1, step_bias.shape[0]), F32),
            pltpu.VMEM((1, step_bias.shape[0]), F32),
            pltpu.VMEM((1, step_bias.shape[0]), F32),
            pltpu.VMEM((1, document_starts.shape[0]), jnp.int32),
            pltpu.VMEM((groups, STATE, length), BF16),
            pltpu.VMEM((groups, length, length), BF16),
            pltpu.VMEM((count, 2 * heads, CHUNK), BF16),
            pltpu.VMEM((8, heads), F32),
            pltpu.VMEM((length, 2 * heads), BF16),
            pltpu.VMEM((length, 2 * heads), BF16),
            pltpu.VMEM((length, 2 * heads), BF16),
            pltpu.VMEM((length, 2 * heads), BF16),
            pltpu.VMEM((8, inner), F32),
            pltpu.VMEM((8, inner), F32),
            pltpu.VMEM((coefs, inner), F32),
            pltpu.VMEM(piece, F32),
            pltpu.VMEM(piece, F32),
            pltpu.VMEM(piece, F32),
            pltpu.VMEM((count, length, CHUNK), F32),
            pltpu.VMEM((bits, *piece), BF16),
            pltpu.VMEM((bits, *piece), BF16),
            pltpu.VMEM(piece, BF16),
            pltpu.VMEM(piece, BF16),
            pltpu.VMEM(piece, BF16),
            pltpu.VMEM(piece, BF16),
            pltpu.VMEM((n, 8, heads), F32),
            pltpu.VMEM((8, heads), F32),
            pltpu.VMEM((n, 8, heads), F32),
            pltpu.VMEM((8, heads), F32),
            pltpu.VMEM((m, 8, heads), F32),
            dma((2, n)),
            dma((2, n)),
            dma((2, m)),
            dma((2, bits, count)),
            dma((2, count)),
            dma((2, count)),
            dma((9,)),
        ],
        compiler_params=pltpu.CompilerParams(
            collective_id=0, has_side_effects=True, vmem_limit_bytes=63 * 2**20
        ),
        name="exchange",
    )(
        head_inputs, gate_inputs, write_keys, read_queries, step_logits,
        step_bias[None], decay_log[None], skip_scale[None], document_starts[None],
    )

    tile = min(length, ROWS)
    return pl.pallas_call(
        scale_kernel,
        grid=(length // tile,),
        out_shape=jax.ShapeDtypeStruct((length, inner), BF16),
        in_specs=[
            pl.BlockSpec((tile, inner), lambda i: (i, 0)),
            pl.BlockSpec((tile, 128), lambda i: (i, 0)),
            pl.BlockSpec((1, inner), lambda i: (0, 0)),
        ],
        out_specs=pl.BlockSpec((tile, inner), lambda i: (i, 0)),
        compiler_params=pltpu.CompilerParams(vmem_limit_bytes=20 * 2**20),
        name="scale",
    )(gated, power, norm_gain[None])


def solution(mesh):
    tokens = P(("ctx", "head"), None)
    return jax.shard_map(
        functools.partial(local, mesh.shape["head"], mesh.shape["ctx"]),
        mesh=mesh,
        in_specs=(tokens,) * 5 + (P("head"), P("head"), P("head"), P(), P("ctx")),
        out_specs=tokens,
        check_vma=False,
    )
```

```python
import functools

import jax
import jax.numpy as jnp
from jax import lax
from jax.experimental import pallas as pl
from jax.experimental.pallas import tpu as pltpu
from jax.sharding import PartitionSpec as P

HEAD_DIM = 64
STATE = 128
BLOCK = 256
CHUNK = 256
SKEW = 3
TURN = 3
ROWS = 32
MESH = pl.DeviceIdType.MESH
F32 = jnp.float32
BF16 = jnp.bfloat16


def split_terms(value, terms):
    parts = []
    for _ in range(terms):
        part = value.astype(BF16)
        parts.append(part)
        value = value - part.astype(F32)
    return parts


def widen(table, ref):
    lane = lax.broadcasted_iota(jnp.int32, (table.shape[0], 128), 1)
    per_tile = 128 // HEAD_DIM
    for j in range(ref.shape[1] // 128):
        tile = jnp.broadcast_to(table[:, j * per_tile : j * per_tile + 1], lane.shape)
        for i in range(1, per_tile):
            column = j * per_tile + i
            tile = jnp.where(lane >= i * HEAD_DIM, jnp.broadcast_to(table[:, column : column + 1], lane.shape), tile)
        ref[:, j * 128 : (j + 1) * 128] = tile


def exchange_kernel(
    n, m, groups,
    x_hbm, gate_hbm, b_hbm, c_hbm, logit_hbm, bias_hbm, decay_hbm, skip_hbm, starts_hbm,
    gated_ref, power_ref,
    x_ref, gate_ref, b_ref, c_ref, logit_ref, bias_ref, decay_ref, skip_ref, starts_ref,
    keys_ref, scores_ref, spread_ref, param_ref,
    tail_ref, up_ref, down_ref, out_ref, skips_ref, line_ref, coef_ref,
    own_ref, sum_ref, before_ref, inside_ref,
    step_send, step_recv, fore_send, fore_recv, back_send, back_recv,
    param_in, decay_out, decay_in, hop_out, hop_in,
    param_sems, decay_sems, hop_sems, step_sems, relay_sems, fore_sems, back_sems, load_sems,
):
    ci = lax.axis_index("ctx")
    zi = lax.axis_index("head")
    bits = m.bit_length() - 1
    length, inner = x_ref.shape
    heads = logit_ref.shape[1]
    count = inner // CHUNK
    per_group = count // groups
    chunk_heads = CHUNK // HEAD_DIM

    half = count // max(n, 4)
    first = 2 * half
    second = count - first
    z_turn = max(first, TURN + bits * SKEW + 1)
    c_turn = (n - 1) * SKEW
    c_done = c_turn + bits * SKEW + 1
    assert c_done + half > count - half

    def first_chunk(i):
        return jnp.where(i < half, i, count - first + i)

    def second_chunk(i):
        return half + i

    pairs = (
        (bias_hbm, bias_ref), (decay_hbm, decay_ref), (skip_hbm, skip_ref), (starts_hbm, starts_ref),
        (b_hbm, b_ref), (c_hbm, c_ref), (logit_hbm, logit_ref), (x_hbm, x_ref), (gate_hbm, gate_ref),
    )
    loads = [pltpu.make_async_copy(src, dst, load_sems.at[i]) for i, (src, dst) in enumerate(pairs)]
    for load in loads:
        load.start()

    def z_peer(d):
        return (ci, lax.rem(zi + d, n))

    def ctx_peer(d):
        return (lax.rem(ci + d, m), zi)

    def ctx_partner(j):
        bit = 1 << j
        upper = lax.rem(ci // bit, 2)
        return ci + bit - 2 * bit * upper, upper

    barrier = pltpu.get_barrier_semaphore()
    for d in range(1, n):
        pl.semaphore_signal(barrier, inc=1, device_id=z_peer(d), device_id_type=MESH)
    for d in range(1, m):
        pl.semaphore_signal(barrier, inc=1, device_id=ctx_peer(d), device_id_type=MESH)

    own_heads = bias_ref.shape[1]
    place = jnp.where(
        lax.broadcasted_iota(jnp.int32, (own_heads, heads), 0) + zi * own_heads
        == lax.broadcasted_iota(jnp.int32, (own_heads, heads), 1), 1.0, 0.0
    ).astype(BF16)
    for load in loads[:4]:
        load.wait()
    raw = jnp.concatenate(
        [bias_ref[...], decay_ref[...], skip_ref[...], jnp.zeros((5, own_heads), F32)], axis=0
    )
    placed = jnp.zeros((8, heads), F32)
    for part in split_terms(raw, 3):
        placed = placed + jnp.dot(part, place, preferred_element_type=F32)
    param_ref[...] = placed

    def remote(src, dst, sems, index, device):
        return pltpu.make_async_remote_copy(
            src_ref=src, dst_ref=dst, send_sem=sems.at[(0, *index)], recv_sem=sems.at[(1, *index)],
            device_id=device, device_id_type=MESH,
        )

    param_copies = [
        remote(param_ref, param_in.at[d], param_sems, (d,), z_peer(d)) for d in range(1, n)
    ]
    decay_copies = [
        remote(decay_out, decay_in.at[d], decay_sems, (d,), z_peer(d)) for d in range(1, n)
    ]
    hop_copies = [
        remote(hop_out, hop_in.at[d], hop_sems, (d,), ctx_peer(d)) for d in range(1, m)
    ]
    pl.semaphore_wait(barrier, n - 1 + m - 1)
    for copy in param_copies:
        copy.start()

    row = lax.broadcasted_iota(jnp.int32, (2 * heads, CHUNK), 0)
    lane = lax.broadcasted_iota(jnp.int32, (2 * heads, CHUNK), 1)

    def fill(k, _):
        own = lane // HEAD_DIM + k * chunk_heads
        spread_ref[k] = jnp.where((row == own) | (row == own + heads), 1.0, 0.0).astype(BF16)
        return 0

    lax.fori_loop(0, count, fill, 0)

    offset = lax.rem(zi * length, BLOCK)
    starts = starts_ref[...].astype(F32)
    mine = lax.broadcasted_iota(jnp.int32, starts.shape, 1) == zi * length // BLOCK
    start = jnp.sum(jnp.where(mine, starts, 0.0), axis=1, keepdims=True) - offset.astype(F32)
    start = jnp.where((start < 0.0) | (start >= length), float(length), start)
    row = lax.broadcasted_iota(jnp.int32, (length, length), 0).astype(F32)
    col = lax.broadcasted_iota(jnp.int32, (length, length), 1).astype(F32)
    lower = jnp.where(row >= col, 1.0, 0.0)
    same = jnp.where(row >= start, 1.0, 0.0) == jnp.where(col >= start, 1.0, 0.0)
    allowed = jnp.where(same, lower, 0.0)
    for load in loads[4:7]:
        load.wait()
    for g in range(groups):
        part = slice(g * STATE, (g + 1) * STATE)
        scores = lax.dot_general(
            c_ref[:, part], b_ref[:, part], (((1,), (1,)), ((), ())), preferred_element_type=F32
        )
        scores_ref[g] = jnp.where(allowed > 0.0, scores, 0.0).astype(BF16)
        keys_ref[g] = b_ref[:, part].astype(F32).T.astype(BF16)
    power_ref[...] = jnp.zeros_like(power_ref)

    for copy in param_copies:
        copy.wait()
    params = param_ref[...]
    for d in range(1, n):
        params = params + param_in[d]

    logits = logit_ref[...].astype(F32) + params[0:1]
    step = jnp.maximum(logits, 0.0) + jnp.log1p(jnp.exp(-jnp.abs(logits)))
    rate = -jnp.exp(params[1:2]) * step
    lower = lower.astype(BF16)
    cum = jnp.zeros((length, heads), F32)
    for part in split_terms(rate, 3)[::-1]:
        cum = cum + jnp.dot(lower, part, preferred_element_type=F32)
    last = cum[length - 1 : length]
    middle = cum[length // 2 - 1 : length // 2]
    position = lax.broadcasted_iota(jnp.int32, (length, heads), 0).astype(F32)
    begins = start < length
    carried = jnp.where(begins, 0.0, jnp.exp(last))

    decay_out[...] = jnp.broadcast_to(carried, decay_out.shape)
    for copy in decay_copies:
        copy.start()
    keep = position >= jnp.where(begins, start, 0.0)
    tail = jnp.where(keep, jnp.exp(last - cum), 0.0) * step
    tail_ref[...] = jnp.concatenate(split_terms(tail, 2), axis=1)
    up_ref[...] = jnp.concatenate(split_terms(jnp.exp(cum - middle), 2), axis=1)
    down_ref[...] = jnp.concatenate(split_terms(jnp.exp(middle - cum) * step, 2), axis=1)
    out_ref[...] = jnp.concatenate(
        split_terms(jnp.where(position < start, jnp.exp(cum), 0.0), 2), axis=1
    )
    widen(jnp.broadcast_to(params[2:3], (8, heads)), skips_ref)
    loads[7].wait()
    loads[8].wait()

    def step_copy(j, k):
        return remote(step_send.at[j, k], step_recv.at[j, k], step_sems, (j, k), (ctx_partner(j)[0], zi))

    def relay_copy(j, k):
        arrived = step_recv.at[j, k]
        return remote(arrived, arrived, relay_sems, (j, k), (ctx_partner(0)[0], zi))

    def is_mine(k):
        return lax.rem(k, 2) == lax.rem(ci, 2)

    def send(j, k, value):
        def go():
            sum_ref[k] = value
            step_send[j, k] = value.astype(BF16)
            step_copy(j, k).start()

        if j == bits - 1:
            pl.when(is_last_lower)(go)
        else:
            go()

    def fore_copy(k):
        return remote(fore_send.at[k], fore_recv.at[k], fore_sems, (k,), (ci, lax.rem(zi + 1, n)))

    def back_copy(k):
        return remote(back_send.at[k], back_recv.at[k], back_sems, (k,), (ci, lax.rem(zi + n - 1, n)))

    def channels(k):
        return pl.ds(pl.multiple_of(k * CHUNK, CHUNK), CHUNK)

    def states(k):
        return pl.ds(pl.multiple_of((k // per_group) * STATE, STATE), STATE)

    def line(k, slot):
        return line_ref[slot : slot + 1, channels(k)]

    def coef(k, slot):
        return coef_ref[slot : slot + 1, channels(k)]

    is_last_upper = ctx_partner(bits - 1)[1] == 1
    is_last_lower = ctx_partner(bits - 1)[1] == 0

    def write(k):
        weight = jnp.dot(tail_ref[...], spread_ref[k], preferred_element_type=F32)
        scaled = (x_ref[:, channels(k)].astype(F32) * weight).astype(BF16)
        written = jnp.dot(keys_ref[k // per_group], scaled, preferred_element_type=F32)
        own_ref[k] = written
        return written

    def look(k):
        x = x_ref[:, channels(k)].astype(F32)
        down = jnp.dot(down_ref[...], spread_ref[k], preferred_element_type=F32)
        up = jnp.dot(up_ref[...], spread_ref[k], preferred_element_type=F32)
        inside = jnp.dot(scores_ref[k // per_group], (x * down).astype(BF16), preferred_element_type=F32)
        inside_ref[k] = up * inside + skips_ref[0:1, channels(k)] * x

    def finish(k, with_back):
        incoming = before_ref[k]
        if with_back:
            incoming = incoming + back_recv[k].astype(F32)
        frozen = (fore_recv[k].astype(F32) + line(k, 1) * incoming).astype(BF16)
        outside = jnp.dot(c_ref[:, states(k)], frozen, preferred_element_type=F32)
        weight = jnp.dot(out_ref[...], spread_ref[k], preferred_element_type=F32)
        gate = gate_ref[:, channels(k)].astype(F32)
        gated = (outside * weight + inside_ref[k]) * (gate / (1.0 + jnp.exp(-gate)))
        gated_ref[:, channels(k)] = gated.astype(BF16)
        square = gated * gated
        total = power_ref[...]
        for i in range(CHUNK // 128):
            total = total + square[:, i * 128 : (i + 1) * 128]
        power_ref[...] = total

    fore_at = zi * SKEW
    back_at = (n - 1 - zi) * SKEW
    done_at = jnp.maximum(fore_at, back_at)

    def iteration(t, _):
        @pl.when(t == TURN)
        def _():
            for copy in decay_copies:
                copy.wait()
            own = decay_out[...]
            before = jnp.ones((8, heads), F32)
            after = jnp.ones((8, heads), F32)
            for d in range(1, n):
                got = decay_in[d]
                before = before * jnp.where(zi >= d, got, 1.0)
                after = after * jnp.where(zi >= d, 1.0, got)
            hop_out[...] = before * own * after
            for copy in hop_copies:
                copy.start()
            widen(jnp.concatenate([own[0:1], before[0:1], after[0:1], own[3:8]], axis=0), line_ref)

        @pl.when(t == TURN + SKEW)
        def _():
            for copy in hop_copies:
                copy.wait()
            total = hop_out[...]
            ahead = jnp.ones((8, heads), F32)
            rows = []
            for j in range(bits):
                bit = 1 << j
                is_upper = ctx_partner(j)[1] == 1
                sibling = ctx_partner(j)[0] // bit
                got = jnp.ones((8, heads), F32)
                for d in range(1, m):
                    source = lax.rem(ci + m - d, m)
                    got = got * jnp.where(source // bit == sibling, hop_in[d], 1.0)
                rows.append(jnp.where(is_upper, 1.0, got))
                rows.append(jnp.where(is_upper, total, 1.0))
                rows.append(jnp.where(is_upper, ahead, 0.0))
                ahead = jnp.where(is_upper, ahead * got, ahead)
                total = total * got
            pad = [jnp.zeros((1, heads), F32)] * (coef_ref.shape[0] - len(rows))
            widen(jnp.concatenate([r[0:1] for r in rows] + pad, axis=0), coef_ref)

        @pl.when(t < first)
        def _():
            write(first_chunk(t))


        def fore(k, is_first):
            @pl.when(zi > 0)
            def _():
                fore_copy(k).wait_recv()

            @pl.when(zi == 0)
            def _():
                fore_recv[k] = jnp.zeros_like(fore_recv[k])
                if is_first:
                    fore_send[k] = own_ref[k].astype(BF16)
                    fore_copy(k).start()

            @pl.when((zi > 0) & (zi < n - 1) if is_first else zi < n - 1)
            def _():
                arrived = fore_recv[k].astype(F32)
                if not is_first:
                    arrived = arrived + line(k, 1) * before_ref[k]
                fore_send[k] = (line(k, 0) * arrived + own_ref[k]).astype(BF16)
                fore_copy(k).start()

        def back(k, is_first):
            @pl.when(zi < n - 1)
            def _():
                back_copy(k).wait_recv()

            @pl.when(zi == n - 1)
            def _():
                back_recv[k] = jnp.zeros_like(back_recv[k])
                if is_first:
                    back_send[k] = own_ref[k].astype(BF16)
                    back_copy(k).start()

            @pl.when((zi > 0) & (zi < n - 1) if is_first else zi > 0)
            def _():
                more = line(k, 2) * own_ref[k] if is_first else before_ref[k]
                back_send[k] = (back_recv[k].astype(F32) + more).astype(BF16)
                back_copy(k).start()

        for at, relay in ((fore_at, fore), (back_at, back)):
            s = t - at

            @pl.when((s >= 0) & (s < first))
            def _():
                relay(first_chunk(s), True)

            @pl.when((s >= z_turn) & (s < z_turn + second))
            def _():
                relay(second_chunk(s - z_turn), False)

        def begin(k):
            step_copy(0, k).wait_recv()
            got = step_recv[0, k].astype(F32)
            before_ref[k] = coef(k, 2) * got

            @pl.when(is_mine(k))
            def _():
                send(1, k, sum_ref[k] * coef(k, 0) + coef(k, 1) * got)

        def advance(j, k):
            step_copy(j, k).wait_recv()
            got = step_recv[j, k].astype(F32)

            @pl.when(ctx_partner(j)[1] == 1)
            def _():
                relay_copy(j, k).start()
                before_ref[k] += coef(k, 2 + 3 * j) * got

            if j < bits - 1:
                send(j + 1, k, sum_ref[k] * coef(k, 3 * j) + coef(k, 1 + 3 * j) * got)

        def share(j, k):
            relay_copy(j, k).wait_recv()
            before_ref[k] += coef(k, 2 + 3 * j) * step_recv[j, k].astype(F32)

        for begins_at, chunk, length_of in ((TURN, second_chunk, second), (c_turn, first_chunk, first)):
            for j in range(bits):
                s = t - begins_at - (j + 1) * SKEW
                k = chunk(s)
                inside = (s >= 0) & (s < length_of)
                if j == 0:
                    pl.when(inside)(functools.partial(begin, k))
                    continue
                if j == bits - 1:
                    inside = inside & is_last_upper
                pl.when(inside & is_mine(k))(functools.partial(advance, j, k))
                s = s - 1
                k = chunk(s)
                inside = (s >= 0) & (s < length_of) & (ctx_partner(j)[1] == 1)
                pl.when(inside & jnp.logical_not(is_mine(k)))(functools.partial(share, j, k))

        @pl.when((t >= TURN) & (t < TURN + second))
        def _():
            k = second_chunk(t - TURN)
            send(0, k, line(k, 2) * write(k))

        @pl.when((t >= c_turn) & (t < c_turn + first))
        def _():
            k = first_chunk(t - c_turn)
            value = line(k, 0) * fore_recv[k].astype(F32) + own_ref[k]
            send(0, k, line(k, 2) * value + back_recv[k].astype(F32))

        s = t - z_turn - done_at

        @pl.when((s >= 0) & (s < second))
        def _():
            finish(second_chunk(s), True)

        r = t - c_done

        @pl.when((r >= 0) & (r < first))
        def _():
            finish(first_chunk(r), False)

        @pl.when(t < count)
        def _():
            look(t)

        return 0

    steps = max(z_turn + second + (n - 1) * SKEW, c_done + first)
    lax.fori_loop(0, steps, iteration, 0)

    def drain(k, _):
        step_copy(0, k).wait_send()

        @pl.when(is_mine(k))
        def _():
            for j in range(1, bits - 1):
                step_copy(j, k).wait_send()

            @pl.when(is_last_lower)
            def _():
                step_copy(bits - 1, k).wait_send()

            for j in range(1, bits):
                @pl.when(ctx_partner(j)[1] == 1)
                def _(j=j):
                    relay_copy(j, k).wait_send()

        @pl.when(zi < n - 1)
        def _():
            fore_copy(k).wait_send()

        @pl.when(zi > 0)
        def _():
            back_copy(k).wait_send()

        return 0

    lax.fori_loop(0, count, drain, 0)


def scale_kernel(gated_ref, power_ref, gain_ref, out_hbm, out_ref, sems):
    length, inner = gated_ref.shape
    tiles = sems.shape[0]
    tile = length // tiles
    width = 1024
    copies = []
    for i in range(tiles):
        rows = slice(i * tile, (i + 1) * tile)
        power = jnp.sum(power_ref[rows], axis=1, keepdims=True)
        factor = lax.rsqrt(power / inner + 1e-05)
        for j in range(inner // width):
            part = slice(j * width, (j + 1) * width)
            out_ref[rows, part] = (gated_ref[rows, part].astype(F32) * factor * gain_ref[:, part]).astype(BF16)
        copy = pltpu.make_async_copy(out_ref.at[rows], out_hbm.at[rows], sems.at[i])
        copy.start()
        copies.append(copy)
    for copy in copies:
        copy.wait()


def local(
    n, m,
    head_inputs, gate_inputs, write_keys, read_queries, step_logits,
    step_bias, decay_log, skip_scale, norm_gain, document_starts,
):
    length, inner = head_inputs.shape
    heads = step_logits.shape[1]
    groups = write_keys.shape[1] // STATE
    assert length <= BLOCK and BLOCK % length == 0 and m & (m - 1) == 0 and m > 2 and n > 1
    bits = m.bit_length() - 1
    count = inner // CHUNK
    coefs = -(-3 * bits // 8) * 8
    assert TURN <= SKEW and count % max(n, 4) == 0

    hbm = pl.BlockSpec(memory_space=pltpu.HBM)
    whole = pl.BlockSpec(memory_space=pltpu.VMEM)
    piece = (count, STATE, CHUNK)
    dma = pltpu.SemaphoreType.DMA
    gated, power = pl.pallas_call(
        functools.partial(exchange_kernel, n, m, groups),
        out_shape=(pltpu.VMEM((length, inner), BF16), pltpu.VMEM((length, 128), F32)),
        in_specs=[hbm] * 9,
        out_specs=(whole, whole),
        scratch_shapes=[
            pltpu.VMEM((length, inner), BF16),
            pltpu.VMEM((length, inner), BF16),
            pltpu.VMEM(write_keys.shape, BF16),
            pltpu.VMEM(read_queries.shape, BF16),
            pltpu.VMEM(step_logits.shape, BF16),
            pltpu.VMEM((1, step_bias.shape[0]), F32),
            pltpu.VMEM((1, step_bias.shape[0]), F32),
            pltpu.VMEM((1, step_bias.shape[0]), F32),
            pltpu.VMEM((1, document_starts.shape[0]), jnp.int32),
            pltpu.VMEM((groups, STATE, length), BF16),
            pltpu.VMEM((groups, length, length), BF16),
            pltpu.VMEM((count, 2 * heads, CHUNK), BF16),
            pltpu.VMEM((8, heads), F32),
            pltpu.VMEM((length, 2 * heads), BF16),
            pltpu.VMEM((length, 2 * heads), BF16),
            pltpu.VMEM((length, 2 * heads), BF16),
            pltpu.VMEM((length, 2 * heads), BF16),
            pltpu.VMEM((8, inner), F32),
            pltpu.VMEM((8, inner), F32),
            pltpu.VMEM((coefs, inner), F32),
            pltpu.VMEM(piece, F32),
            pltpu.VMEM(piece, F32),
            pltpu.VMEM(piece, F32),
            pltpu.VMEM((count, length, CHUNK), F32),
            pltpu.VMEM((bits, *piece), BF16),
            pltpu.VMEM((bits, *piece), BF16),
            pltpu.VMEM(piece, BF16),
            pltpu.VMEM(piece, BF16),
            pltpu.VMEM(piece, BF16),
            pltpu.VMEM(piece, BF16),
            pltpu.VMEM((n, 8, heads), F32),
            pltpu.VMEM((8, heads), F32),
            pltpu.VMEM((n, 8, heads), F32),
            pltpu.VMEM((8, heads), F32),
            pltpu.VMEM((m, 8, heads), F32),
            dma((2, n)),
            dma((2, n)),
            dma((2, m)),
            dma((2, bits, count)),
            dma((2, bits, count)),
            dma((2, count)),
            dma((2, count)),
            dma((9,)),
        ],
        compiler_params=pltpu.CompilerParams(
            collective_id=0, has_side_effects=True, vmem_limit_bytes=58 * 2**20
        ),
        name="exchange",
    )(
        head_inputs, gate_inputs, write_keys, read_queries, step_logits,
        step_bias[None], decay_log[None], skip_scale[None], document_starts[None],
    )

    return pl.pallas_call(
        scale_kernel,
        out_shape=jax.ShapeDtypeStruct((length, inner), BF16),
        in_specs=[whole] * 3,
        out_specs=pl.BlockSpec(memory_space=pl.ANY),
        scratch_shapes=[pltpu.VMEM((length, inner), BF16), dma((length // ROWS,))],
        compiler_params=pltpu.CompilerParams(vmem_limit_bytes=20 * 2**20),
        name="scale",
    )(gated, power, norm_gain[None])


def solution(mesh):
    tokens = P(("ctx", "head"), None)
    return jax.shard_map(
        functools.partial(local, mesh.shape["head"], mesh.shape["ctx"]),
        mesh=mesh,
        in_specs=(tokens,) * 5 + (P("head"), P("head"), P("head"), P(), P("ctx")),
        out_specs=tokens,
        check_vma=False,
    )
```

```python
import functools

import jax
import jax.numpy as jnp
from jax import lax
from jax.experimental import pallas as pl
from jax.experimental.pallas import tpu as pltpu
from jax.sharding import PartitionSpec as P

HEAD_DIM = 64
STATE = 128
BLOCK = 256
CHUNK = 256
SKEW = 3
TURN = 6
ROWS = 32
MESH = pl.DeviceIdType.MESH
F32 = jnp.float32
BF16 = jnp.bfloat16


def split_terms(value, terms):
    parts = []
    for _ in range(terms):
        part = value.astype(BF16)
        parts.append(part)
        value = value - part.astype(F32)
    return parts


def widen(table, ref):
    lane = lax.broadcasted_iota(jnp.int32, (table.shape[0], 128), 1)
    per_tile = 128 // HEAD_DIM
    for j in range(ref.shape[1] // 128):
        tile = jnp.broadcast_to(table[:, j * per_tile : j * per_tile + 1], lane.shape)
        for i in range(1, per_tile):
            column = j * per_tile + i
            tile = jnp.where(lane >= i * HEAD_DIM, jnp.broadcast_to(table[:, column : column + 1], lane.shape), tile)
        ref[:, j * 128 : (j + 1) * 128] = tile


def exchange_kernel(
    n, m, groups,
    x_hbm, gate_hbm, gain_hbm, b_hbm, c_hbm, logit_hbm, bias_hbm, decay_hbm, skip_hbm, starts_hbm,
    gated_ref, power_ref,
    x_ref, gate_ref, gain_ref, b_ref, c_ref, logit_ref, bias_ref, decay_ref, skip_ref, starts_ref,
    keys_ref, scores_ref, spread_ref, param_ref,
    tail_ref, up_ref, down_ref, out_ref, line_ref, coef_ref,
    own_ref, sum_ref, before_ref, inside_ref,
    step_send, step_recv, fore_send, fore_recv, back_send, back_recv,
    param_in, decay_out, decay_in, hop_out, hop_in,
    param_sems, decay_sems, hop_sems, step_sems, relay_sems, fore_sems, back_sems, sent_sems, load_sems,
):
    ci = lax.axis_index("ctx")
    zi = lax.axis_index("head")
    bits = m.bit_length() - 1
    length, inner = x_ref.shape
    heads = logit_ref.shape[1]
    count = inner // CHUNK
    per_group = count // groups
    chunk_heads = CHUNK // HEAD_DIM

    half = count // max(n, 4)
    first = 2 * half
    second = count - first
    hops = [SKEW] + [SKEW * (j + 1) - 1 for j in range(1, bits)]
    z_turn = max(first, TURN + hops[-1] + 2)
    c_turn = half + (n - 1) * SKEW
    c_done = c_turn + hops[-1] + 1
    last_turn = max(z_turn + (n - 1) * SKEW, c_done)
    look_turn = last_turn - count // 2
    both = min(first, second)
    assert look_turn > SKEW and count % 2 == 0
    assert SKEW < TURN <= 2 * SKEW and TURN - SKEW <= half

    def first_chunk(i):
        return jnp.where(i < half, i, count - first + i)

    def second_chunk(i):
        return half + i

    pairs = (
        (bias_hbm, bias_ref), (decay_hbm, decay_ref), (skip_hbm, skip_ref), (starts_hbm, starts_ref),
        (b_hbm, b_ref), (c_hbm, c_ref), (logit_hbm, logit_ref), (x_hbm, x_ref), (gate_hbm, gate_ref),
        (gain_hbm, gain_ref),
    )
    loads = [pltpu.make_async_copy(src, dst, load_sems.at[i]) for i, (src, dst) in enumerate(pairs)]
    for load in loads[:-2]:
        load.start()

    def z_peer(d):
        return (ci, lax.rem(zi + d, n))

    def ctx_peer(d):
        return (lax.rem(ci + d, m), zi)

    def ctx_partner(j):
        bit = 1 << j
        upper = lax.rem(ci // bit, 2)
        return ci + bit - 2 * bit * upper, upper

    barrier = pltpu.get_barrier_semaphore()
    for d in range(1, n):
        pl.semaphore_signal(barrier, inc=1, device_id=z_peer(d), device_id_type=MESH)
    for d in range(1, m):
        pl.semaphore_signal(barrier, inc=1, device_id=ctx_peer(d), device_id_type=MESH)

    own_heads = bias_ref.shape[1]
    place = jnp.where(
        lax.broadcasted_iota(jnp.int32, (own_heads, heads), 0) + zi * own_heads
        == lax.broadcasted_iota(jnp.int32, (own_heads, heads), 1), 1.0, 0.0
    ).astype(BF16)

    def start_in_block():
        offset = lax.rem(zi * length, BLOCK)
        starts = starts_ref[...].astype(F32)
        mine = lax.broadcasted_iota(jnp.int32, starts.shape, 1) == zi * length // BLOCK
        start = jnp.sum(jnp.where(mine, starts, 0.0), axis=1, keepdims=True) - offset.astype(F32)
        return jnp.where((start < 0.0) | (start >= length), float(length), start)

    def decays(params):
        logits = logit_ref[...].astype(F32) + params[0:1]
        step = jnp.maximum(logits, 0.0) + jnp.log1p(jnp.exp(-jnp.abs(logits)))
        rate = -jnp.exp(params[1:2]) * step
        row = lax.broadcasted_iota(jnp.int32, (length, length), 0)
        col = lax.broadcasted_iota(jnp.int32, (length, length), 1)
        lower = jnp.where(row >= col, 1.0, 0.0).astype(BF16)
        cum = jnp.zeros((length, heads), F32)
        for part in split_terms(rate, 3)[::-1]:
            cum = cum + jnp.dot(lower, part, preferred_element_type=F32)
        last = cum[length - 1 : length]
        position = lax.broadcasted_iota(jnp.int32, (length, heads), 0).astype(F32)
        start = start_in_block()
        begins = start < length
        carried = jnp.where(begins, 0.0, jnp.exp(last))
        keep = position >= jnp.where(begins, start, 0.0)
        tail = jnp.where(keep, jnp.exp(last - cum), 0.0) * step
        tail_ref[...] = jnp.concatenate(split_terms(tail, 2), axis=1)
        return step, cum, carried, position, start

    for load in loads[:4]:
        load.wait()
    raw = jnp.concatenate(
        [bias_ref[...], decay_ref[...], skip_ref[...], jnp.zeros((5, own_heads), F32)], axis=0
    )
    placed = jnp.zeros((8, heads), F32)
    for part in split_terms(raw, 3):
        placed = placed + jnp.dot(part, place, preferred_element_type=F32)
    loads[6].wait()
    early = decays(placed)[2]
    owner = lax.broadcasted_iota(jnp.int32, (1, heads), 1) // own_heads == zi
    param_ref[...] = jnp.concatenate(
        [placed[0:3], jnp.where(owner, early, 0.0), placed[4:8]], axis=0
    )

    def remote(src, dst, sems, index, device, sent=None):
        return pltpu.make_async_remote_copy(
            src_ref=src, dst_ref=dst, send_sem=sems.at[(0, *index)] if sent is None else sent_sems.at[sent],
            recv_sem=sems.at[(1, *index)] if sent is None else sems.at[index],
            device_id=device, device_id_type=MESH,
        )

    param_copies = [
        remote(param_ref, param_in.at[d], param_sems, (d,), z_peer(d)) for d in range(1, n)
    ]
    decay_copies = [
        remote(decay_out, decay_in.at[d], decay_sems, (d,), z_peer(d)) for d in range(1, n)
    ]
    hop_copies = [
        remote(hop_out, hop_in.at[d], hop_sems, (d,), ctx_peer(d)) for d in range(1, m)
    ]
    row = lax.broadcasted_iota(jnp.int32, (heads, CHUNK), 0)
    lane = lax.broadcasted_iota(jnp.int32, (heads, CHUNK), 1)

    def fill(k, _):
        spread = jnp.where(row == lane // HEAD_DIM + k * chunk_heads, 1.0, 0.0).astype(BF16)
        spread_ref[k, :heads] = spread
        spread_ref[k, heads:] = spread
        return 0

    def turn_keys(g):
        keys_ref[g] = b_ref[:, g * STATE : (g + 1) * STATE].astype(F32).T.astype(BF16)

    bases = (0, count - half)
    soon = {k // per_group for base in bases for k in range(base, base + SKEW)}
    for base in bases:
        lax.fori_loop(base, base + SKEW, fill, 0)
    loads[4].wait()
    for g in sorted(soon):
        turn_keys(g)
    power_ref[...] = jnp.zeros_like(power_ref)
    pl.semaphore_wait(barrier, n - 1 + m - 1)
    for copy in param_copies:
        copy.start()
    for load in loads[-2:]:
        load.start()
    loads[7].wait()

    def settle():
        lax.fori_loop(0, count, fill, 0)
        for g in range(groups):
            if g not in soon:
                turn_keys(g)
        start = start_in_block()
        row = lax.broadcasted_iota(jnp.int32, (length, length), 0).astype(F32)
        col = lax.broadcasted_iota(jnp.int32, (length, length), 1).astype(F32)
        lower = jnp.where(row >= col, 1.0, 0.0)
        same = jnp.where(row >= start, 1.0, 0.0) == jnp.where(col >= start, 1.0, 0.0)
        allowed = jnp.where(same, lower, 0.0)
        loads[5].wait()
        for g in range(groups):
            part = slice(g * STATE, (g + 1) * STATE)
            scores = lax.dot_general(
                c_ref[:, part], b_ref[:, part], (((1,), (1,)), ((), ())), preferred_element_type=F32
            )
            scores_ref[g] = jnp.where(allowed > 0.0, scores, 0.0).astype(BF16)

        for copy in param_copies:
            copy.wait()
        params = param_ref[...]
        for d in range(1, n):
            params = params + param_in[d]
        step, cum, carried, position, start = decays(params)
        decay_out[...] = jnp.broadcast_to(carried, decay_out.shape)
        for copy in decay_copies:
            copy.start()
        middle = cum[length // 2 - 1 : length // 2]
        up_ref[...] = jnp.concatenate(split_terms(jnp.exp(cum - middle), 2), axis=1)
        down_ref[...] = jnp.concatenate(split_terms(jnp.exp(middle - cum) * step, 2), axis=1)
        out_ref[...] = jnp.concatenate(
            split_terms(jnp.where(position < start, jnp.exp(cum), 0.0), 2), axis=1
        )
        rest = jnp.zeros((4, heads), F32)
        widen(jnp.concatenate([carried, carried, params[3:4], params[2:3], rest], axis=0), line_ref)
        loads[8].wait()
        loads[9].wait()

    def step_copy(j, k):
        return remote(step_send.at[j, k], step_recv.at[j, k], step_sems, (j, k), (ctx_partner(j)[0], zi), j)

    def relay_copy(j, k):
        arrived = step_recv.at[j, k]
        return remote(arrived, arrived, relay_sems, (j, k), (ctx_partner(0)[0], zi), bits + j)

    def is_mine(k):
        return lax.rem(k, 2) == lax.rem(ci, 2)

    def send(j, k, value):
        def go():
            sum_ref[k] = value
            step_send[j, k] = value.astype(BF16)
            step_copy(j, k).start()

        if j == bits - 1:
            pl.when(is_last_lower)(go)
        else:
            go()

    def fore_copy(k):
        return remote(fore_send.at[k], fore_recv.at[k], fore_sems, (k,), (ci, lax.rem(zi + 1, n)), 2 * bits)

    def back_copy(k):
        return remote(back_send.at[k], back_recv.at[k], back_sems, (k,), (ci, lax.rem(zi + n - 1, n)), 2 * bits + 1)

    def channels(k):
        return pl.ds(pl.multiple_of(k * CHUNK, CHUNK), CHUNK)

    def states(k):
        return pl.ds(pl.multiple_of((k // per_group) * STATE, STATE), STATE)

    def line(k, slot):
        return line_ref[slot : slot + 1, channels(k)]

    def coef(k, slot):
        return coef_ref[slot : slot + 1, channels(k)]

    is_last_upper = ctx_partner(bits - 1)[1] == 1
    is_last_lower = ctx_partner(bits - 1)[1] == 0

    def write(k):
        weight = jnp.dot(tail_ref[...], spread_ref[k], preferred_element_type=F32)
        scaled = (x_ref[:, channels(k)].astype(F32) * weight).astype(BF16)
        written = jnp.dot(keys_ref[k // per_group], scaled, preferred_element_type=F32)
        own_ref[k] = written
        return written

    def look(*chunks):
        inputs = [x_ref[:, channels(k)].astype(F32) for k in chunks]
        downs = [jnp.dot(down_ref[...], spread_ref[k], preferred_element_type=F32) for k in chunks]
        pulled = [(x * down).astype(BF16) for x, down in zip(inputs, downs)]
        ups = [jnp.dot(up_ref[...], spread_ref[k], preferred_element_type=F32) for k in chunks]
        insides = [
            jnp.dot(scores_ref[k // per_group], p, preferred_element_type=F32)
            for k, p in zip(chunks, pulled)
        ]
        for k, x, up, inside in zip(chunks, inputs, ups, insides):
            inside_ref[k] = up * inside + line(k, 3) * x

    def finish(*pairs):
        frozens = []
        for k, with_back in pairs:
            incoming = before_ref[k]
            if with_back:
                incoming = incoming + back_recv[k].astype(F32)
            frozens.append((fore_recv[k].astype(F32) + line(k, 1) * incoming).astype(BF16))
        for (k, _), frozen in zip(pairs, frozens):
            weight = jnp.dot(out_ref[...], spread_ref[k], preferred_element_type=F32)
            outside = jnp.dot(c_ref[:, states(k)], frozen, preferred_element_type=F32)
            half_gate = 0.5 * gate_ref[:, channels(k)].astype(F32)
            gated = (outside * weight + inside_ref[k]) * (half_gate * (1.0 + jnp.tanh(half_gate)))
            gated_ref[:, channels(k)] = (gated * gain_ref[:, channels(k)]).astype(BF16)
            square = gated * gated
            total = power_ref[...]
            for i in range(CHUNK // 128):
                total = total + square[:, i * 128 : (i + 1) * 128]
            power_ref[...] = total

    fore_at = zi * SKEW
    back_at = (n - 1 - zi) * SKEW
    head_at = jnp.minimum(fore_at, back_at + half)
    rear_at = jnp.minimum(back_at, fore_at + half)

    def iteration(t, _):
        pl.when(t == SKEW)(settle)

        @pl.when(t == TURN)
        def _():
            for copy in decay_copies:
                copy.wait()
            own = decay_out[...]
            before = jnp.ones((8, heads), F32)
            after = jnp.ones((8, heads), F32)
            for d in range(1, n):
                got = decay_in[d]
                before = before * jnp.where(zi >= d, got, 1.0)
                after = after * jnp.where(zi >= d, 1.0, got)
            hop_out[...] = before * own * after
            for copy in hop_copies:
                copy.start()
            skip = param_ref[2:3]
            for d in range(1, n):
                skip = skip + param_in[d, 2:3]
            widen(jnp.concatenate([own[0:1], before[0:1], after[0:1], skip, own[4:8]], axis=0), line_ref)

        @pl.when(t == TURN + hops[0])
        def _():
            for copy in hop_copies:
                copy.wait()
            total = hop_out[...]
            ahead = jnp.ones((8, heads), F32)
            rows = []
            for j in range(bits):
                bit = 1 << j
                is_upper = ctx_partner(j)[1] == 1
                sibling = ctx_partner(j)[0] // bit
                got = jnp.ones((8, heads), F32)
                for d in range(1, m):
                    source = lax.rem(ci + m - d, m)
                    got = got * jnp.where(source // bit == sibling, hop_in[d], 1.0)
                rows.append(jnp.where(is_upper, 1.0, got))
                rows.append(jnp.where(is_upper, total, 1.0))
                rows.append(jnp.where(is_upper, ahead, 0.0))
                ahead = jnp.where(is_upper, ahead * got, ahead)
                total = total * got
            pad = [jnp.zeros((1, heads), F32)] * (coef_ref.shape[0] - len(rows))
            widen(jnp.concatenate([r[0:1] for r in rows] + pad, axis=0), coef_ref)

        for at, base in ((head_at, 0), (rear_at, count - half)):
            @pl.when((t >= at) & (t < at + half))
            def _(at=at, base=base):
                write(base + t - at)


        def fore(k, is_first):
            @pl.when(zi > 0)
            def _():
                fore_copy(k).wait_recv()

            @pl.when(zi == 0)
            def _():
                fore_recv[k] = jnp.zeros_like(fore_recv[k])
                if is_first:
                    fore_send[k] = own_ref[k].astype(BF16)
                    fore_copy(k).start()

            @pl.when((zi > 0) & (zi < n - 1) if is_first else zi < n - 1)
            def _():
                arrived = fore_recv[k].astype(F32)
                if not is_first:
                    arrived = arrived + line(k, 1) * before_ref[k]
                fore_send[k] = (line(k, 0) * arrived + own_ref[k]).astype(BF16)
                fore_copy(k).start()

        def back(k, is_first):
            @pl.when(zi < n - 1)
            def _():
                back_copy(k).wait_recv()

            @pl.when(zi == n - 1)
            def _():
                back_recv[k] = jnp.zeros_like(back_recv[k])
                if is_first:
                    back_send[k] = own_ref[k].astype(BF16)
                    back_copy(k).start()

            @pl.when((zi > 0) & (zi < n - 1) if is_first else zi > 0)
            def _():
                more = line(k, 2) * own_ref[k] if is_first else before_ref[k]
                back_send[k] = (back_recv[k].astype(F32) + more).astype(BF16)
                back_copy(k).start()

        for at, relay, turned in ((fore_at, fore, 0), (back_at, back, half)):
            s = t - at

            @pl.when((s >= 0) & (s < first))
            def _():
                relay(first_chunk(lax.rem(s + turned, first)), True)

            @pl.when((s >= z_turn) & (s < z_turn + second))
            def _():
                relay(second_chunk(s - z_turn), False)

        def begin(k):
            step_copy(0, k).wait_recv()
            got = step_recv[0, k].astype(F32)
            before_ref[k] = coef(k, 2) * got

            @pl.when(is_mine(k))
            def _():
                send(1, k, sum_ref[k] * coef(k, 0) + coef(k, 1) * got)

        def advance(j, k):
            step_copy(j, k).wait_recv()
            got = step_recv[j, k].astype(F32)

            @pl.when(ctx_partner(j)[1] == 1)
            def _():
                relay_copy(j, k).start()
                before_ref[k] += coef(k, 2 + 3 * j) * got

            if j < bits - 1:
                send(j + 1, k, sum_ref[k] * coef(k, 3 * j) + coef(k, 1 + 3 * j) * got)

        def share(j, k):
            relay_copy(j, k).wait_recv()
            before_ref[k] += coef(k, 2 + 3 * j) * step_recv[j, k].astype(F32)

        for begins_at, chunk, length_of in ((TURN, second_chunk, second), (c_turn, first_chunk, first)):
            for j in range(bits):
                s = t - begins_at - hops[j]
                k = chunk(s)
                inside = (s >= 0) & (s < length_of)
                if j == 0:
                    pl.when(inside)(functools.partial(begin, k))
                    continue
                if j == bits - 1:
                    inside = inside & is_last_upper
                pl.when(inside & is_mine(k))(functools.partial(advance, j, k))
                s = s - 1
                k = chunk(s)
                inside = (s >= 0) & (s < length_of) & (ctx_partner(j)[1] == 1)
                pl.when(inside & jnp.logical_not(is_mine(k)))(functools.partial(share, j, k))

        @pl.when((t >= TURN) & (t < TURN + second))
        def _():
            k = second_chunk(t - TURN)
            send(0, k, line(k, 2) * write(k))

        @pl.when((t >= c_turn) & (t < c_turn + first))
        def _():
            k = first_chunk(t - c_turn)
            value = line(k, 0) * fore_recv[k].astype(F32) + own_ref[k]
            send(0, k, line(k, 2) * value + back_recv[k].astype(F32))

        s = t - last_turn

        @pl.when((s >= 0) & (s < both))
        def _():
            finish((second_chunk(s), True), (first_chunk(s), False))

        if second > both:
            @pl.when((s >= both) & (s < second))
            def _():
                finish((second_chunk(s), True))

        if first > both:
            @pl.when((s >= both) & (s < first))
            def _():
                finish((first_chunk(s), False))

        k = (t - look_turn) * 2

        @pl.when((k >= 0) & (k < count))
        def _():
            look(k, k + 1)

        return 0

    steps = last_turn + max(first, second)
    lax.fori_loop(0, steps, iteration, 0)

    def drain(part, sent):
        pltpu.make_async_copy(part, part, sent_sems.at[sent]).wait()

    drain(step_send.at[0], 0)
    for j in range(1, bits):
        is_upper = ctx_partner(j)[1] == 1

        @pl.when(is_upper)
        def _(j=j):
            drain(step_recv.at[j, : count // 2], bits + j)

        if j < bits - 1:
            drain(step_send.at[j, : count // 2], j)
        else:
            @pl.when(jnp.logical_not(is_upper))
            def _(j=j):
                drain(step_send.at[j, : count // 2], j)

    @pl.when(zi < n - 1)
    def _():
        drain(fore_send, 2 * bits)

    @pl.when(zi > 0)
    def _():
        drain(back_send, 2 * bits + 1)


def scale_kernel(gated_ref, power_ref, out_hbm, out_ref, sems):
    length, inner = gated_ref.shape
    tiles = sems.shape[0]
    tile = length // tiles
    width = 1024
    copies = []
    for i in range(tiles):
        rows = slice(i * tile, (i + 1) * tile)
        power = jnp.sum(power_ref[rows], axis=1, keepdims=True)
        factor = lax.rsqrt(power / inner + 1e-05)
        for j in range(inner // width):
            part = slice(j * width, (j + 1) * width)
            out_ref[rows, part] = (gated_ref[rows, part].astype(F32) * factor).astype(BF16)
        copy = pltpu.make_async_copy(out_ref.at[rows], out_hbm.at[rows], sems.at[i])
        copy.start()
        copies.append(copy)
    for copy in copies:
        copy.wait()


def local(
    n, m,
    head_inputs, gate_inputs, write_keys, read_queries, step_logits,
    step_bias, decay_log, skip_scale, norm_gain, document_starts,
):
    length, inner = head_inputs.shape
    heads = step_logits.shape[1]
    groups = write_keys.shape[1] // STATE
    assert length <= BLOCK and BLOCK % length == 0 and m & (m - 1) == 0 and m > 2 and n > 1
    bits = m.bit_length() - 1
    count = inner // CHUNK
    coefs = -(-3 * bits // 8) * 8
    assert count % max(n, 4) == 0

    hbm = pl.BlockSpec(memory_space=pltpu.HBM)
    whole = pl.BlockSpec(memory_space=pltpu.VMEM)
    piece = (count, STATE, CHUNK)
    dma = pltpu.SemaphoreType.DMA
    gated, power = pl.pallas_call(
        functools.partial(exchange_kernel, n, m, groups),
        out_shape=(pltpu.VMEM((length, inner), BF16), pltpu.VMEM((length, 128), F32)),
        in_specs=[hbm] * 10,
        out_specs=(whole, whole),
        scratch_shapes=[
            pltpu.VMEM((length, inner), BF16),
            pltpu.VMEM((length, inner), BF16),
            pltpu.VMEM((1, inner), F32),
            pltpu.VMEM(write_keys.shape, BF16),
            pltpu.VMEM(read_queries.shape, BF16),
            pltpu.VMEM(step_logits.shape, BF16),
            pltpu.VMEM((1, step_bias.shape[0]), F32),
            pltpu.VMEM((1, step_bias.shape[0]), F32),
            pltpu.VMEM((1, step_bias.shape[0]), F32),
            pltpu.VMEM((1, document_starts.shape[0]), jnp.int32),
            pltpu.VMEM((groups, STATE, length), BF16),
            pltpu.VMEM((groups, length, length), BF16),
            pltpu.VMEM((count, 2 * heads, CHUNK), BF16),
            pltpu.VMEM((8, heads), F32),
            pltpu.VMEM((length, 2 * heads), BF16),
            pltpu.VMEM((length, 2 * heads), BF16),
            pltpu.VMEM((length, 2 * heads), BF16),
            pltpu.VMEM((length, 2 * heads), BF16),
            pltpu.VMEM((8, inner), F32),
            pltpu.VMEM((coefs, inner), F32),
            pltpu.VMEM(piece, F32),
            pltpu.VMEM(piece, F32),
            pltpu.VMEM(piece, F32),
            pltpu.VMEM((count, length, CHUNK), F32),
            pltpu.VMEM((bits, *piece), BF16),
            pltpu.VMEM((bits, *piece), BF16),
            pltpu.VMEM(piece, BF16),
            pltpu.VMEM(piece, BF16),
            pltpu.VMEM(piece, BF16),
            pltpu.VMEM(piece, BF16),
            pltpu.VMEM((n, 8, heads), F32),
            pltpu.VMEM((8, heads), F32),
            pltpu.VMEM((n, 8, heads), F32),
            pltpu.VMEM((8, heads), F32),
            pltpu.VMEM((m, 8, heads), F32),
            dma((2, n)),
            dma((2, n)),
            dma((2, m)),
            dma((bits, count)),
            dma((bits, count)),
            dma((count,)),
            dma((count,)),
            dma((2 * bits + 2,)),
            dma((10,)),
        ],
        compiler_params=pltpu.CompilerParams(
            collective_id=0, has_side_effects=True, vmem_limit_bytes=58 * 2**20
        ),
        name="exchange",
    )(
        head_inputs, gate_inputs, norm_gain[None], write_keys, read_queries, step_logits,
        step_bias[None], decay_log[None], skip_scale[None], document_starts[None],
    )

    return pl.pallas_call(
        scale_kernel,
        out_shape=jax.ShapeDtypeStruct((length, inner), BF16),
        in_specs=[whole] * 2,
        out_specs=pl.BlockSpec(memory_space=pl.ANY),
        scratch_shapes=[pltpu.VMEM((length, inner), BF16), dma((length // ROWS,))],
        compiler_params=pltpu.CompilerParams(vmem_limit_bytes=20 * 2**20),
        name="scale",
    )(gated, power)


def solution(mesh):
    tokens = P(("ctx", "head"), None)
    return jax.shard_map(
        functools.partial(local, mesh.shape["head"], mesh.shape["ctx"]),
        mesh=mesh,
        in_specs=(tokens,) * 5 + (P("head"), P("head"), P("head"), P(), P("ctx")),
        out_specs=tokens,
        check_vma=False,
    )
```

```python
import functools

import jax
import jax.numpy as jnp
from jax import lax
from jax.experimental import pallas as pl
from jax.experimental.pallas import tpu as pltpu
from jax.sharding import PartitionSpec as P

HEAD_DIM = 64
STATE = 128
BLOCK = 256
CHUNK = 256
SKEW = 3
TURN = 6
LEAD = 9
ROWS = 32
MESH = pl.DeviceIdType.MESH
F32 = jnp.float32
BF16 = jnp.bfloat16


def split_terms(value, terms):
    parts = []
    for _ in range(terms):
        part = value.astype(BF16)
        parts.append(part)
        value = value - part.astype(F32)
    return parts


def widen(table, ref):
    lane = lax.broadcasted_iota(jnp.int32, (table.shape[0], 128), 1)
    per_tile = 128 // HEAD_DIM
    for j in range(ref.shape[1] // 128):
        tile = jnp.broadcast_to(table[:, j * per_tile : j * per_tile + 1], lane.shape)
        for i in range(1, per_tile):
            column = j * per_tile + i
            tile = jnp.where(lane >= i * HEAD_DIM, jnp.broadcast_to(table[:, column : column + 1], lane.shape), tile)
        ref[:, j * 128 : (j + 1) * 128] = tile


def exchange_kernel(
    n, m, groups,
    x_hbm, gate_hbm, gain_hbm, b_hbm, c_hbm, logit_hbm, bias_hbm, decay_hbm, skip_hbm, starts_hbm,
    gated_ref, power_ref,
    x_ref, gate_ref, gain_ref, b_ref, c_ref, logit_ref, bias_ref, decay_ref, skip_ref, starts_ref,
    keys_ref, scores_ref, spread_ref, param_ref,
    tail_ref, up_ref, down_ref, out_ref, line_ref, coef_ref,
    own_ref, sum_ref, before_ref, inside_ref,
    step_send, step_recv, fore_send, fore_recv, back_send, back_recv,
    param_in, decay_out, decay_in, hop_out, hop_in,
    param_sems, decay_sems, hop_sems, step_sems, relay_sems, fore_sems, back_sems, sent_sems, load_sems,
):
    ci = lax.axis_index("ctx")
    zi = lax.axis_index("head")
    bits = m.bit_length() - 1
    length, inner = x_ref.shape
    heads = logit_ref.shape[1]
    count = inner // CHUNK
    per_group = count // groups
    chunk_heads = CHUNK // HEAD_DIM

    half = count // max(n, 4)
    first = 2 * half
    second = count - first
    hops = [SKEW * (j + 1) - 1 for j in range(bits)]
    z_turn = max(first, TURN + hops[-1] + 2)
    c_turn = half + (n - 1) * SKEW
    c_done = c_turn + hops[-1] + 1
    last_turn = max(z_turn + (n - 1) * SKEW, c_done)
    look_turn = last_turn - LEAD
    both = min(first, second)
    assert look_turn > SKEW
    assert SKEW < TURN <= 2 * SKEW and TURN - SKEW <= half

    def first_chunk(i):
        return jnp.where(i < half, i, count - first + i)

    def second_chunk(i):
        return half + i

    pairs = (
        (bias_hbm, bias_ref), (decay_hbm, decay_ref), (skip_hbm, skip_ref), (starts_hbm, starts_ref),
        (b_hbm, b_ref), (c_hbm, c_ref), (logit_hbm, logit_ref), (x_hbm, x_ref), (gate_hbm, gate_ref),
        (gain_hbm, gain_ref),
    )
    loads = [pltpu.make_async_copy(src, dst, load_sems.at[i]) for i, (src, dst) in enumerate(pairs)]
    for load in loads[:-2]:
        load.start()

    def z_peer(d):
        return (ci, lax.rem(zi + d, n))

    def ctx_peer(d):
        return (lax.rem(ci + d, m), zi)

    def ctx_partner(j):
        bit = 1 << j
        upper = lax.rem(ci // bit, 2)
        return ci + bit - 2 * bit * upper, upper

    barrier = pltpu.get_barrier_semaphore()
    for d in range(1, n):
        pl.semaphore_signal(barrier, inc=1, device_id=z_peer(d), device_id_type=MESH)
    for d in range(1, m):
        pl.semaphore_signal(barrier, inc=1, device_id=ctx_peer(d), device_id_type=MESH)

    own_heads = bias_ref.shape[1]
    place = jnp.where(
        lax.broadcasted_iota(jnp.int32, (own_heads, heads), 0) + zi * own_heads
        == lax.broadcasted_iota(jnp.int32, (own_heads, heads), 1), 1.0, 0.0
    ).astype(BF16)

    def start_in_block():
        offset = lax.rem(zi * length, BLOCK)
        starts = starts_ref[...].astype(F32)
        mine = lax.broadcasted_iota(jnp.int32, starts.shape, 1) == zi * length // BLOCK
        start = jnp.sum(jnp.where(mine, starts, 0.0), axis=1, keepdims=True) - offset.astype(F32)
        return jnp.where((start < 0.0) | (start >= length), float(length), start)

    def decays(params):
        logits = logit_ref[...].astype(F32) + params[0:1]
        step = jnp.maximum(logits, 0.0) + jnp.log1p(jnp.exp(-jnp.abs(logits)))
        rate = -jnp.exp(params[1:2]) * step
        row = lax.broadcasted_iota(jnp.int32, (length, length), 0)
        col = lax.broadcasted_iota(jnp.int32, (length, length), 1)
        lower = jnp.where(row >= col, 1.0, 0.0).astype(BF16)
        cum = jnp.zeros((length, heads), F32)
        for part in split_terms(rate, 3)[::-1]:
            cum = cum + jnp.dot(lower, part, preferred_element_type=F32)
        last = cum[length - 1 : length]
        position = lax.broadcasted_iota(jnp.int32, (length, heads), 0).astype(F32)
        start = start_in_block()
        begins = start < length
        carried = jnp.where(begins, 0.0, jnp.exp(last))
        keep = position >= jnp.where(begins, start, 0.0)
        tail = jnp.where(keep, jnp.exp(last - cum), 0.0) * step
        tail_ref[...] = jnp.concatenate(split_terms(tail, 2), axis=1)
        return step, cum, carried, position, start

    for load in loads[:4]:
        load.wait()
    raw = jnp.concatenate(
        [bias_ref[...], decay_ref[...], skip_ref[...], jnp.zeros((5, own_heads), F32)], axis=0
    )
    placed = jnp.zeros((8, heads), F32)
    for part in split_terms(raw, 3):
        placed = placed + jnp.dot(part, place, preferred_element_type=F32)
    loads[6].wait()
    early = decays(placed)[2]
    owner = lax.broadcasted_iota(jnp.int32, (1, heads), 1) // own_heads == zi
    param_ref[...] = jnp.concatenate(
        [placed[0:3], jnp.where(owner, early, 0.0), placed[4:8]], axis=0
    )

    def remote(src, dst, sems, index, device, sent=None):
        return pltpu.make_async_remote_copy(
            src_ref=src, dst_ref=dst, send_sem=sems.at[(0, *index)] if sent is None else sent_sems.at[sent],
            recv_sem=sems.at[(1, *index)] if sent is None else sems.at[index],
            device_id=device, device_id_type=MESH,
        )

    param_copies = [
        remote(param_ref, param_in.at[d], param_sems, (d,), z_peer(d)) for d in range(1, n)
    ]
    decay_copies = [
        remote(decay_out, decay_in.at[d], decay_sems, (d,), z_peer(d)) for d in range(1, n)
    ]
    hop_copies = [
        remote(hop_out, hop_in.at[d], hop_sems, (d,), ctx_peer(d)) for d in range(1, m)
    ]
    row = lax.broadcasted_iota(jnp.int32, (heads, CHUNK), 0)
    lane = lax.broadcasted_iota(jnp.int32, (heads, CHUNK), 1)

    def fill(k, _):
        spread = jnp.where(row == lane // HEAD_DIM + k * chunk_heads, 1.0, 0.0).astype(BF16)
        spread_ref[k, :heads] = spread
        spread_ref[k, heads:] = spread
        return 0

    def turn_keys(g):
        keys_ref[g] = b_ref[:, g * STATE : (g + 1) * STATE].astype(F32).T.astype(BF16)

    bases = (0, count - half)
    soon = {k // per_group for base in bases for k in range(base, base + SKEW)}
    for base in bases:
        lax.fori_loop(base, base + SKEW, fill, 0)
    loads[4].wait()
    for g in sorted(soon):
        turn_keys(g)
    power_ref[...] = jnp.zeros_like(power_ref)
    pl.semaphore_wait(barrier, n - 1 + m - 1)
    for copy in param_copies:
        copy.start()
    for load in loads[-2:]:
        load.start()
    loads[7].wait()

    def settle():
        lax.fori_loop(0, count, fill, 0)
        for g in range(groups):
            if g not in soon:
                turn_keys(g)
        start = start_in_block()
        row = lax.broadcasted_iota(jnp.int32, (length, length), 0).astype(F32)
        col = lax.broadcasted_iota(jnp.int32, (length, length), 1).astype(F32)
        lower = jnp.where(row >= col, 1.0, 0.0)
        same = jnp.where(row >= start, 1.0, 0.0) == jnp.where(col >= start, 1.0, 0.0)
        allowed = jnp.where(same, lower, 0.0)
        loads[5].wait()
        for g in range(groups):
            part = slice(g * STATE, (g + 1) * STATE)
            scores = lax.dot_general(
                c_ref[:, part], b_ref[:, part], (((1,), (1,)), ((), ())), preferred_element_type=F32
            )
            scores_ref[g] = jnp.where(allowed > 0.0, scores, 0.0).astype(BF16)

        for copy in param_copies:
            copy.wait()
        params = param_ref[...]
        for d in range(1, n):
            params = params + param_in[d]
        step, cum, carried, position, start = decays(params)
        decay_out[...] = jnp.broadcast_to(carried, decay_out.shape)
        for copy in decay_copies:
            copy.start()
        middle = cum[length // 2 - 1 : length // 2]
        up_ref[...] = jnp.concatenate(split_terms(jnp.exp(cum - middle), 2), axis=1)
        down_ref[...] = jnp.concatenate(split_terms(jnp.exp(middle - cum) * step, 2), axis=1)
        out_ref[...] = jnp.concatenate(
            split_terms(jnp.where(position < start, jnp.exp(cum), 0.0), 2), axis=1
        )
        rest = jnp.zeros((4, heads), F32)
        widen(jnp.concatenate([carried, carried, params[3:4], params[2:3], rest], axis=0), line_ref)
        loads[8].wait()
        loads[9].wait()

    def step_copy(j, k):
        return remote(step_send.at[j, k], step_recv.at[j, k], step_sems, (j, k), (ctx_partner(j)[0], zi), j)

    def relay_copy(j, k):
        arrived = step_recv.at[j, k]
        return remote(arrived, arrived, relay_sems, (j, k), (ctx_partner(0)[0], zi), bits + j)

    def is_mine(k):
        return lax.rem(k, 2) == lax.rem(ci, 2)

    def send(j, k, value):
        def go():
            sum_ref[k] = value
            step_send[j, k] = value.astype(BF16)
            step_copy(j, k).start()

        if j == bits - 1:
            pl.when(is_last_lower)(go)
        else:
            go()

    def fore_copy(k):
        return remote(fore_send.at[k], fore_recv.at[k], fore_sems, (k,), (ci, lax.rem(zi + 1, n)), 2 * bits)

    def back_copy(k):
        return remote(back_send.at[k], back_recv.at[k], back_sems, (k,), (ci, lax.rem(zi + n - 1, n)), 2 * bits + 1)

    def channels(k):
        return pl.ds(pl.multiple_of(k * CHUNK, CHUNK), CHUNK)

    def states(k):
        return pl.ds(pl.multiple_of((k // per_group) * STATE, STATE), STATE)

    def line(k, slot):
        return line_ref[slot : slot + 1, channels(k)]

    def coef(k, slot):
        return coef_ref[slot : slot + 1, channels(k)]

    is_last_upper = ctx_partner(bits - 1)[1] == 1
    is_last_lower = ctx_partner(bits - 1)[1] == 0

    def write(k):
        weight = jnp.dot(tail_ref[...], spread_ref[k], preferred_element_type=F32)
        scaled = (x_ref[:, channels(k)].astype(F32) * weight).astype(BF16)
        written = jnp.dot(keys_ref[k // per_group], scaled, preferred_element_type=F32)
        own_ref[k] = written
        return written

    def look(*chunks):
        inputs = [x_ref[:, channels(k)].astype(F32) for k in chunks]
        downs = [jnp.dot(down_ref[...], spread_ref[k], preferred_element_type=F32) for k in chunks]
        pulled = [(x * down).astype(BF16) for x, down in zip(inputs, downs)]
        ups = [jnp.dot(up_ref[...], spread_ref[k], preferred_element_type=F32) for k in chunks]
        insides = [
            jnp.dot(scores_ref[k // per_group], p, preferred_element_type=F32)
            for k, p in zip(chunks, pulled)
        ]
        for k, x, up, inside in zip(chunks, inputs, ups, insides):
            inside_ref[k] = up * inside + line(k, 3) * x

    def finish(*pairs):
        frozens = []
        for k, with_back in pairs:
            incoming = before_ref[k]
            if with_back:
                incoming = incoming + back_recv[k].astype(F32)
            frozens.append((fore_recv[k].astype(F32) + line(k, 1) * incoming).astype(BF16))
        for (k, _), frozen in zip(pairs, frozens):
            weight = jnp.dot(out_ref[...], spread_ref[k], preferred_element_type=F32)
            outside = jnp.dot(c_ref[:, states(k)], frozen, preferred_element_type=F32)
            half_gate = 0.5 * gate_ref[:, channels(k)].astype(F32)
            gated = (outside * weight + inside_ref[k]) * (half_gate * (1.0 + jnp.tanh(half_gate)))
            gated_ref[:, channels(k)] = (gated * gain_ref[:, channels(k)]).astype(BF16)
            square = gated * gated
            total = power_ref[...]
            for i in range(CHUNK // 128):
                total = total + square[:, i * 128 : (i + 1) * 128]
            power_ref[...] = total

    fore_at = zi * SKEW
    back_at = (n - 1 - zi) * SKEW
    head_at = jnp.minimum(fore_at, back_at + half)
    rear_at = jnp.minimum(back_at, fore_at + half)

    def iteration(t, _):
        pl.when(t == SKEW)(settle)

        @pl.when(t == TURN)
        def _():
            for copy in decay_copies:
                copy.wait()
            own = decay_out[...]
            before = jnp.ones((8, heads), F32)
            after = jnp.ones((8, heads), F32)
            for d in range(1, n):
                got = decay_in[d]
                before = before * jnp.where(zi >= d, got, 1.0)
                after = after * jnp.where(zi >= d, 1.0, got)
            hop_out[...] = before * own * after
            for copy in hop_copies:
                copy.start()
            skip = param_ref[2:3]
            for d in range(1, n):
                skip = skip + param_in[d, 2:3]
            widen(jnp.concatenate([own[0:1], before[0:1], after[0:1], skip, own[4:8]], axis=0), line_ref)

        @pl.when(t == TURN + hops[0])
        def _():
            for copy in hop_copies:
                copy.wait()
            total = hop_out[...]
            ahead = jnp.ones((8, heads), F32)
            rows = []
            for j in range(bits):
                bit = 1 << j
                is_upper = ctx_partner(j)[1] == 1
                sibling = ctx_partner(j)[0] // bit
                got = jnp.ones((8, heads), F32)
                for d in range(1, m):
                    source = lax.rem(ci + m - d, m)
                    got = got * jnp.where(source // bit == sibling, hop_in[d], 1.0)
                rows.append(jnp.where(is_upper, 1.0, got))
                rows.append(jnp.where(is_upper, total, 1.0))
                rows.append(jnp.where(is_upper, ahead, 0.0))
                ahead = jnp.where(is_upper, ahead * got, ahead)
                total = total * got
            pad = [jnp.zeros((1, heads), F32)] * (coef_ref.shape[0] - len(rows))
            widen(jnp.concatenate([r[0:1] for r in rows] + pad, axis=0), coef_ref)

        for at, base in ((head_at, 0), (rear_at, count - half)):
            @pl.when((t >= at) & (t < at + half))
            def _(at=at, base=base):
                write(base + t - at)


        def fore(k, is_first):
            @pl.when(zi > 0)
            def _():
                fore_copy(k).wait_recv()

            @pl.when(zi == 0)
            def _():
                fore_recv[k] = jnp.zeros_like(fore_recv[k])
                if is_first:
                    fore_send[k] = own_ref[k].astype(BF16)
                    fore_copy(k).start()

            @pl.when((zi > 0) & (zi < n - 1) if is_first else zi < n - 1)
            def _():
                arrived = fore_recv[k].astype(F32)
                if not is_first:
                    arrived = arrived + line(k, 1) * before_ref[k]
                fore_send[k] = (line(k, 0) * arrived + own_ref[k]).astype(BF16)
                fore_copy(k).start()

        def back(k, is_first):
            @pl.when(zi < n - 1)
            def _():
                back_copy(k).wait_recv()

            @pl.when(zi == n - 1)
            def _():
                back_recv[k] = jnp.zeros_like(back_recv[k])
                if is_first:
                    back_send[k] = own_ref[k].astype(BF16)
                    back_copy(k).start()

            @pl.when((zi > 0) & (zi < n - 1) if is_first else zi > 0)
            def _():
                more = line(k, 2) * own_ref[k] if is_first else before_ref[k]
                back_send[k] = (back_recv[k].astype(F32) + more).astype(BF16)
                back_copy(k).start()

        for at, relay, turned in ((fore_at, fore, 0), (back_at, back, half)):
            s = t - at

            @pl.when((s >= 0) & (s < first))
            def _():
                relay(first_chunk(lax.rem(s + turned, first)), True)

            @pl.when((s >= z_turn) & (s < z_turn + second))
            def _():
                relay(second_chunk(s - z_turn), False)

        def begin(k):
            step_copy(0, k).wait_recv()
            got = step_recv[0, k].astype(F32)
            before_ref[k] = coef(k, 2) * got

            @pl.when(is_mine(k))
            def _():
                send(1, k, sum_ref[k] * coef(k, 0) + coef(k, 1) * got)

        def advance(j, k):
            step_copy(j, k).wait_recv()
            got = step_recv[j, k].astype(F32)

            @pl.when(ctx_partner(j)[1] == 1)
            def _():
                relay_copy(j, k).start()
                before_ref[k] += coef(k, 2 + 3 * j) * got

            if j < bits - 1:
                send(j + 1, k, sum_ref[k] * coef(k, 3 * j) + coef(k, 1 + 3 * j) * got)

        def share(j, k):
            relay_copy(j, k).wait_recv()
            before_ref[k] += coef(k, 2 + 3 * j) * step_recv[j, k].astype(F32)

        for begins_at, chunk, length_of in ((TURN, second_chunk, second), (c_turn, first_chunk, first)):
            for j in range(bits):
                s = t - begins_at - hops[j]
                k = chunk(s)
                inside = (s >= 0) & (s < length_of)
                if j == 0:
                    pl.when(inside)(functools.partial(begin, k))
                    continue
                if j == bits - 1:
                    inside = inside & is_last_upper
                pl.when(inside & is_mine(k))(functools.partial(advance, j, k))
                s = s - 1
                k = chunk(s)
                inside = (s >= 0) & (s < length_of) & (ctx_partner(j)[1] == 1)
                pl.when(inside & jnp.logical_not(is_mine(k)))(functools.partial(share, j, k))

        @pl.when((t >= TURN) & (t < TURN + second))
        def _():
            k = second_chunk(t - TURN)
            send(0, k, line(k, 2) * write(k))

        @pl.when((t >= c_turn) & (t < c_turn + first))
        def _():
            k = first_chunk(t - c_turn)
            value = line(k, 0) * fore_recv[k].astype(F32) + own_ref[k]
            send(0, k, line(k, 2) * value + back_recv[k].astype(F32))

        s = t - last_turn

        @pl.when((s >= 0) & (s < both))
        def _():
            finish((second_chunk(s), True), (first_chunk(s), False))

        if second > both:
            @pl.when((s >= both) & (s < second))
            def _():
                finish((second_chunk(s), True))

        if first > both:
            @pl.when((s >= both) & (s < first))
            def _():
                finish((first_chunk(s), False))

        s = t - look_turn

        @pl.when((s >= 0) & (s < both))
        def _():
            look(second_chunk(s), first_chunk(s))

        if first != second:
            rest = second_chunk if second > both else first_chunk

            @pl.when((s >= both) & (s < max(first, second)))
            def _():
                look(rest(s))

        return 0

    steps = last_turn + max(first, second)
    lax.fori_loop(0, steps, iteration, 0)

    def drain(part, sent):
        pltpu.make_async_copy(part, part, sent_sems.at[sent]).wait()

    drain(step_send.at[0], 0)
    for j in range(1, bits):
        is_upper = ctx_partner(j)[1] == 1

        @pl.when(is_upper)
        def _(j=j):
            drain(step_recv.at[j, : count // 2], bits + j)

        if j < bits - 1:
            drain(step_send.at[j, : count // 2], j)
        else:
            @pl.when(jnp.logical_not(is_upper))
            def _(j=j):
                drain(step_send.at[j, : count // 2], j)

    @pl.when(zi < n - 1)
    def _():
        drain(fore_send, 2 * bits)

    @pl.when(zi > 0)
    def _():
        drain(back_send, 2 * bits + 1)


def scale_kernel(gated_ref, power_ref, out_hbm, out_ref, sems):
    length, inner = gated_ref.shape
    tiles = sems.shape[0]
    tile = length // tiles
    width = 1024
    copies = []
    for i in range(tiles):
        rows = slice(i * tile, (i + 1) * tile)
        power = jnp.sum(power_ref[rows], axis=1, keepdims=True)
        factor = lax.rsqrt(power / inner + 1e-05)
        for j in range(inner // width):
            part = slice(j * width, (j + 1) * width)
            out_ref[rows, part] = (gated_ref[rows, part].astype(F32) * factor).astype(BF16)
        copy = pltpu.make_async_copy(out_ref.at[rows], out_hbm.at[rows], sems.at[i])
        copy.start()
        copies.append(copy)
    for copy in copies:
        copy.wait()


def local(
    n, m,
    head_inputs, gate_inputs, write_keys, read_queries, step_logits,
    step_bias, decay_log, skip_scale, norm_gain, document_starts,
):
    length, inner = head_inputs.shape
    heads = step_logits.shape[1]
    groups = write_keys.shape[1] // STATE
    assert length <= BLOCK and BLOCK % length == 0 and m & (m - 1) == 0 and m > 2 and n > 1
    bits = m.bit_length() - 1
    count = inner // CHUNK
    coefs = -(-3 * bits // 8) * 8
    assert count % max(n, 4) == 0

    hbm = pl.BlockSpec(memory_space=pltpu.HBM)
    whole = pl.BlockSpec(memory_space=pltpu.VMEM)
    piece = (count, STATE, CHUNK)
    dma = pltpu.SemaphoreType.DMA
    gated, power = pl.pallas_call(
        functools.partial(exchange_kernel, n, m, groups),
        out_shape=(pltpu.VMEM((length, inner), BF16), pltpu.VMEM((length, 128), F32)),
        in_specs=[hbm] * 10,
        out_specs=(whole, whole),
        scratch_shapes=[
            pltpu.VMEM((length, inner), BF16),
            pltpu.VMEM((length, inner), BF16),
            pltpu.VMEM((1, inner), F32),
            pltpu.VMEM(write_keys.shape, BF16),
            pltpu.VMEM(read_queries.shape, BF16),
            pltpu.VMEM(step_logits.shape, BF16),
            pltpu.VMEM((1, step_bias.shape[0]), F32),
            pltpu.VMEM((1, step_bias.shape[0]), F32),
            pltpu.VMEM((1, step_bias.shape[0]), F32),
            pltpu.VMEM((1, document_starts.shape[0]), jnp.int32),
            pltpu.VMEM((groups, STATE, length), BF16),
            pltpu.VMEM((groups, length, length), BF16),
            pltpu.VMEM((count, 2 * heads, CHUNK), BF16),
            pltpu.VMEM((8, heads), F32),
            pltpu.VMEM((length, 2 * heads), BF16),
            pltpu.VMEM((length, 2 * heads), BF16),
            pltpu.VMEM((length, 2 * heads), BF16),
            pltpu.VMEM((length, 2 * heads), BF16),
            pltpu.VMEM((8, inner), F32),
            pltpu.VMEM((coefs, inner), F32),
            pltpu.VMEM(piece, F32),
            pltpu.VMEM(piece, F32),
            pltpu.VMEM(piece, F32),
            pltpu.VMEM((count, length, CHUNK), F32),
            pltpu.VMEM((bits, *piece), BF16),
            pltpu.VMEM((bits, *piece), BF16),
            pltpu.VMEM(piece, BF16),
            pltpu.VMEM(piece, BF16),
            pltpu.VMEM(piece, BF16),
            pltpu.VMEM(piece, BF16),
            pltpu.VMEM((n, 8, heads), F32),
            pltpu.VMEM((8, heads), F32),
            pltpu.VMEM((n, 8, heads), F32),
            pltpu.VMEM((8, heads), F32),
            pltpu.VMEM((m, 8, heads), F32),
            dma((2, n)),
            dma((2, n)),
            dma((2, m)),
            dma((bits, count)),
            dma((bits, count)),
            dma((count,)),
            dma((count,)),
            dma((2 * bits + 2,)),
            dma((10,)),
        ],
        compiler_params=pltpu.CompilerParams(
            collective_id=0, has_side_effects=True, vmem_limit_bytes=58 * 2**20
        ),
        name="exchange",
    )(
        head_inputs, gate_inputs, norm_gain[None], write_keys, read_queries, step_logits,
        step_bias[None], decay_log[None], skip_scale[None], document_starts[None],
    )

    return pl.pallas_call(
        scale_kernel,
        out_shape=jax.ShapeDtypeStruct((length, inner), BF16),
        in_specs=[whole] * 2,
        out_specs=pl.BlockSpec(memory_space=pl.ANY),
        scratch_shapes=[pltpu.VMEM((length, inner), BF16), dma((length // ROWS,))],
        compiler_params=pltpu.CompilerParams(vmem_limit_bytes=20 * 2**20),
        name="scale",
    )(gated, power)


def solution(mesh):
    tokens = P(("ctx", "head"), None)
    return jax.shard_map(
        functools.partial(local, mesh.shape["head"], mesh.shape["ctx"]),
        mesh=mesh,
        in_specs=(tokens,) * 5 + (P("head"), P("head"), P("head"), P(), P("ctx")),
        out_specs=tokens,
        check_vma=False,
    )
```

```python
import functools

import jax
import jax.numpy as jnp
from jax import lax
from jax.experimental import pallas as pl
from jax.experimental.pallas import tpu as pltpu
from jax.sharding import PartitionSpec as P

HEAD_DIM = 64
STATE = 128
BLOCK = 256
CHUNK = 256
SKEW = 3
TURN = 6
LEAD = 9
ROWS = 32
MESH = pl.DeviceIdType.MESH
F32 = jnp.float32
BF16 = jnp.bfloat16


def split_terms(value, terms):
    parts = []
    for _ in range(terms):
        part = value.astype(BF16)
        parts.append(part)
        value = value - part.astype(F32)
    return parts


def widen(table, ref):
    lane = lax.broadcasted_iota(jnp.int32, (table.shape[0], 128), 1)
    per_tile = 128 // HEAD_DIM
    for j in range(ref.shape[1] // 128):
        tile = jnp.broadcast_to(table[:, j * per_tile : j * per_tile + 1], lane.shape)
        for i in range(1, per_tile):
            column = j * per_tile + i
            tile = jnp.where(lane >= i * HEAD_DIM, jnp.broadcast_to(table[:, column : column + 1], lane.shape), tile)
        ref[:, j * 128 : (j + 1) * 128] = tile


def exchange_kernel(
    n, m, groups,
    x_hbm, gate_hbm, gain_hbm, b_hbm, c_hbm, logit_hbm, bias_hbm, decay_hbm, skip_hbm, starts_hbm,
    gated_ref, power_ref,
    x_ref, gate_ref, gain_ref, b_ref, c_ref, logit_ref, bias_ref, decay_ref, skip_ref, starts_ref,
    keys_ref, scores_ref, spread_ref, param_ref,
    tail_ref, up_ref, down_ref, out_ref, line_ref, coef_ref,
    own_ref, sum_ref, before_ref, inside_ref,
    step_send, step_recv, fore_send, fore_recv, back_send, back_recv,
    param_in, decay_out, decay_in, hop_out, hop_in,
    param_sems, decay_sems, hop_sems, step_sems, relay_sems, fore_sems, back_sems, sent_sems, load_sems,
):
    ci = lax.axis_index("ctx")
    zi = lax.axis_index("head")
    bits = m.bit_length() - 1
    length, inner = x_ref.shape
    heads = logit_ref.shape[1]
    count = inner // CHUNK
    per_group = count // groups
    chunk_heads = CHUNK // HEAD_DIM

    half = count // max(n, 4)
    first = 2 * half
    second = count - first
    hops = [SKEW * (j + 1) - 1 for j in range(bits)]
    fast = hops[:-1] + [hops[-1] - 1]
    z_turn = max(first, TURN + hops[-1] + 2)
    c_turn = half + (n - 1) * SKEW
    c_done = c_turn + fast[-1] + 1
    last_turn = max(z_turn + (n - 1) * SKEW, c_done) + 1
    look_turn = last_turn - LEAD
    both = min(first, second)
    assert look_turn > SKEW
    assert SKEW < TURN <= 2 * SKEW and TURN - SKEW <= half

    def first_chunk(i):
        return jnp.where(i < half, i, count - first + i)

    def second_chunk(i):
        return half + i

    pairs = (
        (bias_hbm, bias_ref), (decay_hbm, decay_ref), (skip_hbm, skip_ref), (starts_hbm, starts_ref),
        (b_hbm, b_ref), (c_hbm, c_ref), (logit_hbm, logit_ref), (x_hbm, x_ref), (gate_hbm, gate_ref),
        (gain_hbm, gain_ref),
    )
    loads = [pltpu.make_async_copy(src, dst, load_sems.at[i]) for i, (src, dst) in enumerate(pairs)]
    for load in loads[:-2]:
        load.start()

    def z_peer(d):
        return (ci, lax.rem(zi + d, n))

    def ctx_peer(d):
        return (lax.rem(ci + d, m), zi)

    def ctx_partner(j):
        bit = 1 << j
        upper = lax.rem(ci // bit, 2)
        return ci + bit - 2 * bit * upper, upper

    barrier = pltpu.get_barrier_semaphore()
    for d in range(1, n):
        pl.semaphore_signal(barrier, inc=1, device_id=z_peer(d), device_id_type=MESH)
    for d in range(1, m):
        pl.semaphore_signal(barrier, inc=1, device_id=ctx_peer(d), device_id_type=MESH)

    own_heads = bias_ref.shape[1]
    place = jnp.where(
        lax.broadcasted_iota(jnp.int32, (own_heads, heads), 0) + zi * own_heads
        == lax.broadcasted_iota(jnp.int32, (own_heads, heads), 1), 1.0, 0.0
    ).astype(BF16)

    def start_in_block():
        offset = lax.rem(zi * length, BLOCK)
        starts = starts_ref[...].astype(F32)
        mine = lax.broadcasted_iota(jnp.int32, starts.shape, 1) == zi * length // BLOCK
        start = jnp.sum(jnp.where(mine, starts, 0.0), axis=1, keepdims=True) - offset.astype(F32)
        return jnp.where((start < 0.0) | (start >= length), float(length), start)

    def decays(params):
        logits = logit_ref[...].astype(F32) + params[0:1]
        step = jnp.maximum(logits, 0.0) + jnp.log1p(jnp.exp(-jnp.abs(logits)))
        rate = -jnp.exp(params[1:2]) * step
        row = lax.broadcasted_iota(jnp.int32, (length, length), 0)
        col = lax.broadcasted_iota(jnp.int32, (length, length), 1)
        lower = jnp.where(row >= col, 1.0, 0.0).astype(BF16)
        cum = jnp.zeros((length, heads), F32)
        for part in split_terms(rate, 3)[::-1]:
            cum = cum + jnp.dot(lower, part, preferred_element_type=F32)
        last = cum[length - 1 : length]
        position = lax.broadcasted_iota(jnp.int32, (length, heads), 0).astype(F32)
        start = start_in_block()
        begins = start < length
        carried = jnp.where(begins, 0.0, jnp.exp(last))
        keep = position >= jnp.where(begins, start, 0.0)
        tail = jnp.where(keep, jnp.exp(last - cum), 0.0) * step
        tail_ref[...] = jnp.concatenate(split_terms(tail, 2), axis=1)
        return step, cum, carried, position, start

    for load in loads[:4]:
        load.wait()
    raw = jnp.concatenate(
        [bias_ref[...], decay_ref[...], skip_ref[...], jnp.zeros((5, own_heads), F32)], axis=0
    )
    placed = jnp.zeros((8, heads), F32)
    for part in split_terms(raw, 3):
        placed = placed + jnp.dot(part, place, preferred_element_type=F32)
    loads[6].wait()
    early = decays(placed)[2]
    owner = lax.broadcasted_iota(jnp.int32, (1, heads), 1) // own_heads == zi
    param_ref[...] = jnp.concatenate(
        [placed[0:3], jnp.where(owner, early, 0.0), placed[4:8]], axis=0
    )

    def remote(src, dst, sems, index, device, sent=None):
        return pltpu.make_async_remote_copy(
            src_ref=src, dst_ref=dst, send_sem=sems.at[(0, *index)] if sent is None else sent_sems.at[sent],
            recv_sem=sems.at[(1, *index)] if sent is None else sems.at[index],
            device_id=device, device_id_type=MESH,
        )

    param_copies = [
        remote(param_ref, param_in.at[d], param_sems, (d,), z_peer(d)) for d in range(1, n)
    ]
    decay_copies = [
        remote(decay_out, decay_in.at[d], decay_sems, (d,), z_peer(d)) for d in range(1, n)
    ]
    hop_copies = [
        remote(hop_out, hop_in.at[d], hop_sems, (d,), ctx_peer(d)) for d in range(1, m)
    ]
    row = lax.broadcasted_iota(jnp.int32, (heads, CHUNK), 0)
    lane = lax.broadcasted_iota(jnp.int32, (heads, CHUNK), 1)

    def fill(k, _):
        spread = jnp.where(row == lane // HEAD_DIM + k * chunk_heads, 1.0, 0.0).astype(BF16)
        spread_ref[k, :heads] = spread
        spread_ref[k, heads:] = spread
        return 0

    def turn_keys(g):
        keys_ref[g] = b_ref[:, g * STATE : (g + 1) * STATE].astype(F32).T.astype(BF16)

    bases = (0, count - half)
    soon = {k // per_group for base in bases for k in range(base, base + SKEW)}
    for base in bases:
        lax.fori_loop(base, base + SKEW, fill, 0)
    loads[4].wait()
    for g in sorted(soon):
        turn_keys(g)
    power_ref[...] = jnp.zeros_like(power_ref)
    pl.semaphore_wait(barrier, n - 1 + m - 1)
    for copy in param_copies:
        copy.start()
    for load in loads[-2:]:
        load.start()
    loads[7].wait()

    def settle():
        lax.fori_loop(0, count, fill, 0)
        for g in range(groups):
            if g not in soon:
                turn_keys(g)
        start = start_in_block()
        row = lax.broadcasted_iota(jnp.int32, (length, length), 0).astype(F32)
        col = lax.broadcasted_iota(jnp.int32, (length, length), 1).astype(F32)
        lower = jnp.where(row >= col, 1.0, 0.0)
        same = jnp.where(row >= start, 1.0, 0.0) == jnp.where(col >= start, 1.0, 0.0)
        allowed = jnp.where(same, lower, 0.0)
        loads[5].wait()
        for g in range(groups):
            part = slice(g * STATE, (g + 1) * STATE)
            scores = lax.dot_general(
                c_ref[:, part], b_ref[:, part], (((1,), (1,)), ((), ())), preferred_element_type=F32
            )
            scores_ref[g] = jnp.where(allowed > 0.0, scores, 0.0).astype(BF16)

        for copy in param_copies:
            copy.wait()
        params = param_ref[...]
        for d in range(1, n):
            params = params + param_in[d]
        step, cum, carried, position, start = decays(params)
        decay_out[...] = jnp.broadcast_to(carried, decay_out.shape)
        for copy in decay_copies:
            copy.start()
        middle = cum[length // 2 - 1 : length // 2]
        up_ref[...] = jnp.concatenate(split_terms(jnp.exp(cum - middle), 2), axis=1)
        down_ref[...] = jnp.concatenate(split_terms(jnp.exp(middle - cum) * step, 2), axis=1)
        out_ref[...] = jnp.concatenate(
            split_terms(jnp.where(position < start, jnp.exp(cum), 0.0), 2), axis=1
        )
        rest = jnp.zeros((4, heads), F32)
        widen(jnp.concatenate([carried, carried, params[3:4], params[2:3], rest], axis=0), line_ref)
        loads[8].wait()
        loads[9].wait()

    def step_copy(j, k):
        return remote(step_send.at[j, k], step_recv.at[j, k], step_sems, (j, k), (ctx_partner(j)[0], zi), j)

    def relay_copy(j, k):
        arrived = step_recv.at[j, k]
        return remote(arrived, arrived, relay_sems, (j, k), (ctx_partner(0)[0], zi), bits + j)

    def is_mine(k):
        return lax.rem(k, 2) == lax.rem(ci, 2)

    def send(j, k, value):
        def go():
            sum_ref[k] = value
            step_send[j, k] = value.astype(BF16)
            step_copy(j, k).start()

        if j == bits - 1:
            pl.when(is_last_lower)(go)
        else:
            go()

    def fore_copy(k):
        return remote(fore_send.at[k], fore_recv.at[k], fore_sems, (k,), (ci, lax.rem(zi + 1, n)), 2 * bits)

    def back_copy(k):
        return remote(back_send.at[k], back_recv.at[k], back_sems, (k,), (ci, lax.rem(zi + n - 1, n)), 2 * bits + 1)

    def channels(k):
        return pl.ds(pl.multiple_of(k * CHUNK, CHUNK), CHUNK)

    def states(k):
        return pl.ds(pl.multiple_of((k // per_group) * STATE, STATE), STATE)

    def line(k, slot):
        return line_ref[slot : slot + 1, channels(k)]

    def coef(k, slot):
        return coef_ref[slot : slot + 1, channels(k)]

    is_last_upper = ctx_partner(bits - 1)[1] == 1
    is_last_lower = ctx_partner(bits - 1)[1] == 0

    def write(k):
        weight = jnp.dot(tail_ref[...], spread_ref[k], preferred_element_type=F32)
        scaled = (x_ref[:, channels(k)].astype(F32) * weight).astype(BF16)
        written = jnp.dot(keys_ref[k // per_group], scaled, preferred_element_type=F32)
        own_ref[k] = written
        return written

    def look(*chunks):
        inputs = [x_ref[:, channels(k)].astype(F32) for k in chunks]
        downs = [jnp.dot(down_ref[...], spread_ref[k], preferred_element_type=F32) for k in chunks]
        pulled = [(x * down).astype(BF16) for x, down in zip(inputs, downs)]
        ups = [jnp.dot(up_ref[...], spread_ref[k], preferred_element_type=F32) for k in chunks]
        insides = [
            jnp.dot(scores_ref[k // per_group], p, preferred_element_type=F32)
            for k, p in zip(chunks, pulled)
        ]
        for k, x, up, inside in zip(chunks, inputs, ups, insides):
            inside_ref[k] = up * inside + line(k, 3) * x

    def finish(*pairs):
        frozens = []
        for k, with_back in pairs:
            incoming = before_ref[k]
            if with_back:
                incoming = incoming + back_recv[k].astype(F32)
            frozens.append((fore_recv[k].astype(F32) + line(k, 1) * incoming).astype(BF16))
        for (k, _), frozen in zip(pairs, frozens):
            weight = jnp.dot(out_ref[...], spread_ref[k], preferred_element_type=F32)
            outside = jnp.dot(c_ref[:, states(k)], frozen, preferred_element_type=F32)
            half_gate = 0.5 * gate_ref[:, channels(k)].astype(F32)
            gated = (outside * weight + inside_ref[k]) * (half_gate * (1.0 + jnp.tanh(half_gate)))
            gated_ref[:, channels(k)] = (gated * gain_ref[:, channels(k)]).astype(BF16)
            square = gated * gated
            total = power_ref[...]
            for i in range(CHUNK // 128):
                total = total + square[:, i * 128 : (i + 1) * 128]
            power_ref[...] = total

    fore_at = zi * SKEW
    back_at = (n - 1 - zi) * SKEW
    head_at = jnp.minimum(fore_at, back_at + half)
    rear_at = jnp.minimum(back_at, fore_at + half)

    def iteration(t, _):
        pl.when(t == SKEW)(settle)

        s = t - last_turn

        @pl.when((s >= 0) & (s < both))
        def _():
            finish((second_chunk(s), True), (first_chunk(s), False))

        if second > both:
            @pl.when((s >= both) & (s < second))
            def _():
                finish((second_chunk(s), True))

        if first > both:
            @pl.when((s >= both) & (s < first))
            def _():
                finish((first_chunk(s), False))

        @pl.when(t == TURN)
        def _():
            for copy in decay_copies:
                copy.wait()
            own = decay_out[...]
            before = jnp.ones((8, heads), F32)
            after = jnp.ones((8, heads), F32)
            for d in range(1, n):
                got = decay_in[d]
                before = before * jnp.where(zi >= d, got, 1.0)
                after = after * jnp.where(zi >= d, 1.0, got)
            hop_out[...] = before * own * after
            for copy in hop_copies:
                copy.start()
            skip = param_ref[2:3]
            for d in range(1, n):
                skip = skip + param_in[d, 2:3]
            widen(jnp.concatenate([own[0:1], before[0:1], after[0:1], skip, own[4:8]], axis=0), line_ref)

        @pl.when(t == TURN + hops[0])
        def _():
            for copy in hop_copies:
                copy.wait()
            total = hop_out[...]
            ahead = jnp.ones((8, heads), F32)
            rows = []
            for j in range(bits):
                bit = 1 << j
                is_upper = ctx_partner(j)[1] == 1
                sibling = ctx_partner(j)[0] // bit
                got = jnp.ones((8, heads), F32)
                for d in range(1, m):
                    source = lax.rem(ci + m - d, m)
                    got = got * jnp.where(source // bit == sibling, hop_in[d], 1.0)
                rows.append(jnp.where(is_upper, ahead, 0.0))
                if j < bits - 1:
                    rows.append(jnp.where(is_upper, 1.0, got))
                    rows.append(jnp.where(is_upper, total, 1.0))
                ahead = jnp.where(is_upper, ahead * got, ahead)
                total = total * got
            pad = [jnp.zeros((1, heads), F32)] * (coef_ref.shape[0] - len(rows))
            widen(jnp.concatenate([r[0:1] for r in rows] + pad, axis=0), coef_ref)

        for at, base in ((head_at, 0), (rear_at, count - half)):
            @pl.when((t >= at) & (t < at + half))
            def _(at=at, base=base):
                write(base + t - at)


        def fore(k, is_first):
            @pl.when(zi > 0)
            def _():
                fore_copy(k).wait_recv()

            @pl.when(zi == 0)
            def _():
                fore_recv[k] = jnp.zeros_like(fore_recv[k])
                if is_first:
                    fore_send[k] = own_ref[k].astype(BF16)
                    fore_copy(k).start()

            @pl.when((zi > 0) & (zi < n - 1) if is_first else zi < n - 1)
            def _():
                arrived = fore_recv[k].astype(F32)
                if not is_first:
                    arrived = arrived + line(k, 1) * before_ref[k]
                fore_send[k] = (line(k, 0) * arrived + own_ref[k]).astype(BF16)
                fore_copy(k).start()

        def back(k, is_first):
            @pl.when(zi < n - 1)
            def _():
                back_copy(k).wait_recv()

            @pl.when(zi == n - 1)
            def _():
                back_recv[k] = jnp.zeros_like(back_recv[k])
                if is_first:
                    back_send[k] = own_ref[k].astype(BF16)
                    back_copy(k).start()

            @pl.when((zi > 0) & (zi < n - 1) if is_first else zi > 0)
            def _():
                more = line(k, 2) * own_ref[k] if is_first else before_ref[k]
                back_send[k] = (back_recv[k].astype(F32) + more).astype(BF16)
                back_copy(k).start()

        for at, relay, turned in ((fore_at, fore, 0), (back_at, back, half)):
            s = t - at

            @pl.when((s >= 0) & (s < first))
            def _():
                relay(first_chunk(lax.rem(s + turned, first)), True)

            @pl.when((s >= z_turn) & (s < z_turn + second))
            def _():
                relay(second_chunk(s - z_turn), False)

        def begin(k):
            step_copy(0, k).wait_recv()
            got = step_recv[0, k].astype(F32)
            before_ref[k] = coef(k, 0) * got

            @pl.when(is_mine(k))
            def _():
                send(1, k, sum_ref[k] * coef(k, 1) + coef(k, 2) * got)

        def advance(j, k):
            step_copy(j, k).wait_recv()
            got = step_recv[j, k].astype(F32)

            @pl.when(ctx_partner(j)[1] == 1)
            def _():
                relay_copy(j, k).start()
                before_ref[k] += coef(k, 3 * j) * got

            if j < bits - 1:
                send(j + 1, k, sum_ref[k] * coef(k, 1 + 3 * j) + coef(k, 2 + 3 * j) * got)

        def share(j, k):
            relay_copy(j, k).wait_recv()
            before_ref[k] += coef(k, 3 * j) * step_recv[j, k].astype(F32)

        for begins_at, chunk, length_of, after in (
            (TURN, second_chunk, second, hops), (c_turn, first_chunk, first, fast),
        ):
            for j in range(bits):
                s = t - begins_at - after[j]
                k = chunk(s)
                inside = (s >= 0) & (s < length_of)
                if j == 0:
                    pl.when(inside)(functools.partial(begin, k))
                    continue
                if j == bits - 1:
                    inside = inside & is_last_upper
                pl.when(inside & is_mine(k))(functools.partial(advance, j, k))
                s = s - 1
                k = chunk(s)
                inside = (s >= 0) & (s < length_of) & (ctx_partner(j)[1] == 1)
                pl.when(inside & jnp.logical_not(is_mine(k)))(functools.partial(share, j, k))

        @pl.when((t >= TURN) & (t < TURN + second))
        def _():
            k = second_chunk(t - TURN)
            send(0, k, line(k, 2) * write(k))

        @pl.when((t >= c_turn) & (t < c_turn + first))
        def _():
            k = first_chunk(t - c_turn)
            value = line(k, 0) * fore_recv[k].astype(F32) + own_ref[k]
            send(0, k, line(k, 2) * value + back_recv[k].astype(F32))

        s = t - look_turn

        @pl.when((s >= 0) & (s < both))
        def _():
            look(second_chunk(s), first_chunk(s))

        if first != second:
            rest = second_chunk if second > both else first_chunk

            @pl.when((s >= both) & (s < max(first, second)))
            def _():
                look(rest(s))

        return 0

    steps = last_turn + max(first, second)
    lax.fori_loop(0, steps, iteration, 0)

    def drain(part, sent):
        pltpu.make_async_copy(part, part, sent_sems.at[sent]).wait()

    drain(step_send.at[0], 0)
    for j in range(1, bits):
        is_upper = ctx_partner(j)[1] == 1

        @pl.when(is_upper)
        def _(j=j):
            drain(step_recv.at[j, : count // 2], bits + j)

        if j < bits - 1:
            drain(step_send.at[j, : count // 2], j)
        else:
            @pl.when(jnp.logical_not(is_upper))
            def _(j=j):
                drain(step_send.at[j, : count // 2], j)

    @pl.when(zi < n - 1)
    def _():
        drain(fore_send, 2 * bits)

    @pl.when(zi > 0)
    def _():
        drain(back_send, 2 * bits + 1)


def scale_kernel(gated_ref, power_ref, out_hbm, out_ref, sems):
    length, inner = gated_ref.shape
    tiles = sems.shape[0]
    tile = length // tiles
    width = 1024
    copies = []
    for i in range(tiles):
        rows = slice(i * tile, (i + 1) * tile)
        power = jnp.sum(power_ref[rows], axis=1, keepdims=True)
        factor = lax.rsqrt(power / inner + 1e-05)
        for j in range(inner // width):
            part = slice(j * width, (j + 1) * width)
            out_ref[rows, part] = (gated_ref[rows, part].astype(F32) * factor).astype(BF16)
        copy = pltpu.make_async_copy(out_ref.at[rows], out_hbm.at[rows], sems.at[i])
        copy.start()
        copies.append(copy)
    for copy in copies:
        copy.wait()


def local(
    n, m,
    head_inputs, gate_inputs, write_keys, read_queries, step_logits,
    step_bias, decay_log, skip_scale, norm_gain, document_starts,
):
    length, inner = head_inputs.shape
    heads = step_logits.shape[1]
    groups = write_keys.shape[1] // STATE
    assert length <= BLOCK and BLOCK % length == 0 and m & (m - 1) == 0 and m > 2 and n > 1
    bits = m.bit_length() - 1
    count = inner // CHUNK
    coefs = -(-(3 * bits - 2) // 8) * 8
    assert count % max(n, 4) == 0

    hbm = pl.BlockSpec(memory_space=pltpu.HBM)
    whole = pl.BlockSpec(memory_space=pltpu.VMEM)
    piece = (count, STATE, CHUNK)
    dma = pltpu.SemaphoreType.DMA
    gated, power = pl.pallas_call(
        functools.partial(exchange_kernel, n, m, groups),
        out_shape=(pltpu.VMEM((length, inner), BF16), pltpu.VMEM((length, 128), F32)),
        in_specs=[hbm] * 10,
        out_specs=(whole, whole),
        scratch_shapes=[
            pltpu.VMEM((length, inner), BF16),
            pltpu.VMEM((length, inner), BF16),
            pltpu.VMEM((1, inner), F32),
            pltpu.VMEM(write_keys.shape, BF16),
            pltpu.VMEM(read_queries.shape, BF16),
            pltpu.VMEM(step_logits.shape, BF16),
            pltpu.VMEM((1, step_bias.shape[0]), F32),
            pltpu.VMEM((1, step_bias.shape[0]), F32),
            pltpu.VMEM((1, step_bias.shape[0]), F32),
            pltpu.VMEM((1, document_starts.shape[0]), jnp.int32),
            pltpu.VMEM((groups, STATE, length), BF16),
            pltpu.VMEM((groups, length, length), BF16),
            pltpu.VMEM((count, 2 * heads, CHUNK), BF16),
            pltpu.VMEM((8, heads), F32),
            pltpu.VMEM((length, 2 * heads), BF16),
            pltpu.VMEM((length, 2 * heads), BF16),
            pltpu.VMEM((length, 2 * heads), BF16),
            pltpu.VMEM((length, 2 * heads), BF16),
            pltpu.VMEM((8, inner), F32),
            pltpu.VMEM((coefs, inner), F32),
            pltpu.VMEM(piece, F32),
            pltpu.VMEM(piece, F32),
            pltpu.VMEM(piece, F32),
            pltpu.VMEM((count, length, CHUNK), F32),
            pltpu.VMEM((bits, *piece), BF16),
            pltpu.VMEM((bits, *piece), BF16),
            pltpu.VMEM(piece, BF16),
            pltpu.VMEM(piece, BF16),
            pltpu.VMEM(piece, BF16),
            pltpu.VMEM(piece, BF16),
            pltpu.VMEM((n, 8, heads), F32),
            pltpu.VMEM((8, heads), F32),
            pltpu.VMEM((n, 8, heads), F32),
            pltpu.VMEM((8, heads), F32),
            pltpu.VMEM((m, 8, heads), F32),
            dma((2, n)),
            dma((2, n)),
            dma((2, m)),
            dma((bits, count)),
            dma((bits, count)),
            dma((count,)),
            dma((count,)),
            dma((2 * bits + 2,)),
            dma((10,)),
        ],
        compiler_params=pltpu.CompilerParams(
            collective_id=0, has_side_effects=True, vmem_limit_bytes=58 * 2**20
        ),
        name="exchange",
    )(
        head_inputs, gate_inputs, norm_gain[None], write_keys, read_queries, step_logits,
        step_bias[None], decay_log[None], skip_scale[None], document_starts[None],
    )

    return pl.pallas_call(
        scale_kernel,
        out_shape=jax.ShapeDtypeStruct((length, inner), BF16),
        in_specs=[whole] * 2,
        out_specs=pl.BlockSpec(memory_space=pl.ANY),
        scratch_shapes=[pltpu.VMEM((length, inner), BF16), dma((length // ROWS,))],
        compiler_params=pltpu.CompilerParams(vmem_limit_bytes=20 * 2**20),
        name="scale",
    )(gated, power)


def solution(mesh):
    tokens = P(("ctx", "head"), None)
    return jax.shard_map(
        functools.partial(local, mesh.shape["head"], mesh.shape["ctx"]),
        mesh=mesh,
        in_specs=(tokens,) * 5 + (P("head"), P("head"), P("head"), P(), P("ctx")),
        out_specs=tokens,
        check_vma=False,
    )
```

```python
import functools

import jax
import jax.numpy as jnp
from jax import lax
from jax.experimental import pallas as pl
from jax.experimental.pallas import tpu as pltpu
from jax.sharding import PartitionSpec as P

HEAD_DIM = 64
STATE = 128
BLOCK = 256
CHUNK = 256
SKEW = 3
TURN = 6
LEAD = 9
ROWS = 32
MESH = pl.DeviceIdType.MESH
F32 = jnp.float32
BF16 = jnp.bfloat16


def split_terms(value, terms):
    parts = []
    for _ in range(terms):
        part = value.astype(BF16)
        parts.append(part)
        value = value - part.astype(F32)
    return parts


def widen(table, ref):
    lane = lax.broadcasted_iota(jnp.int32, (table.shape[0], 128), 1)
    per_tile = 128 // HEAD_DIM
    for j in range(ref.shape[1] // 128):
        tile = jnp.broadcast_to(table[:, j * per_tile : j * per_tile + 1], lane.shape)
        for i in range(1, per_tile):
            column = j * per_tile + i
            tile = jnp.where(lane >= i * HEAD_DIM, jnp.broadcast_to(table[:, column : column + 1], lane.shape), tile)
        ref[:, j * 128 : (j + 1) * 128] = tile


def exchange_kernel(
    n, m, groups,
    x_hbm, gate_hbm, gain_hbm, b_hbm, c_hbm, logit_hbm, bias_hbm, decay_hbm, skip_hbm, starts_hbm,
    gated_ref, power_ref,
    x_ref, gate_ref, gain_ref, b_ref, c_ref, logit_ref, bias_ref, decay_ref, skip_ref, starts_ref,
    keys_ref, scores_ref, spread_ref, param_ref,
    tail_ref, up_ref, down_ref, out_ref, line_ref, coef_ref,
    own_ref, sum_ref, before_ref, inside_ref,
    step_send, step_recv, fore_send, fore_recv, back_send, back_recv,
    param_in, decay_out, decay_in, hop_out, hop_in,
    param_sems, decay_sems, hop_sems, step_sems, relay_sems, fore_sems, back_sems, sent_sems, load_sems,
):
    ci = lax.axis_index("ctx")
    zi = lax.axis_index("head")
    bits = m.bit_length() - 1
    length, inner = x_ref.shape
    heads = logit_ref.shape[1]
    count = inner // CHUNK
    per_group = count // groups
    chunk_heads = CHUNK // HEAD_DIM

    half = count // max(n, 4)
    first = 2 * half
    second = count - first
    hops = [SKEW * (j + 1) - 1 for j in range(bits)]
    fast = hops[:-1] + [hops[-1] - 1]
    z_turn = max(first, TURN + hops[-1] + 2)
    c_turn = half + (n - 1) * SKEW
    c_done = c_turn + fast[-1] + 1
    last_turn = max(z_turn + (n - 1) * SKEW, c_done) + 1
    look_turn = last_turn - LEAD
    both = min(first, second)
    assert look_turn > SKEW
    assert SKEW < TURN <= 2 * SKEW and TURN - SKEW <= half

    def first_chunk(i):
        return jnp.where(i < half, i, count - first + i)

    def second_chunk(i):
        return half + i

    pairs = (
        (bias_hbm, bias_ref), (decay_hbm, decay_ref), (skip_hbm, skip_ref), (starts_hbm, starts_ref),
        (b_hbm, b_ref), (c_hbm, c_ref), (logit_hbm, logit_ref), (x_hbm, x_ref), (gate_hbm, gate_ref),
        (gain_hbm, gain_ref),
    )
    loads = [pltpu.make_async_copy(src, dst, load_sems.at[i]) for i, (src, dst) in enumerate(pairs)]
    for load in loads[:-2]:
        load.start()

    def z_peer(d):
        return (ci, lax.rem(zi + d, n))

    def ctx_peer(d):
        return (lax.rem(ci + d, m), zi)

    def ctx_partner(j):
        bit = 1 << j
        upper = lax.rem(ci // bit, 2)
        return ci + bit - 2 * bit * upper, upper

    barrier = pltpu.get_barrier_semaphore()
    for d in range(1, n):
        pl.semaphore_signal(barrier, inc=1, device_id=z_peer(d), device_id_type=MESH)
    for d in range(1, m):
        pl.semaphore_signal(barrier, inc=1, device_id=ctx_peer(d), device_id_type=MESH)

    own_heads = bias_ref.shape[1]
    place = jnp.where(
        lax.broadcasted_iota(jnp.int32, (own_heads, heads), 0) + zi * own_heads
        == lax.broadcasted_iota(jnp.int32, (own_heads, heads), 1), 1.0, 0.0
    ).astype(BF16)

    def start_in_block():
        offset = lax.rem(zi * length, BLOCK)
        starts = starts_ref[...].astype(F32)
        mine = lax.broadcasted_iota(jnp.int32, starts.shape, 1) == zi * length // BLOCK
        start = jnp.sum(jnp.where(mine, starts, 0.0), axis=1, keepdims=True) - offset.astype(F32)
        return jnp.where((start < 0.0) | (start >= length), float(length), start)

    def decays(params):
        logits = logit_ref[...].astype(F32) + params[0:1]
        step = jnp.maximum(logits, 0.0) + jnp.log1p(jnp.exp(-jnp.abs(logits)))
        rate = -jnp.exp(params[1:2]) * step
        row = lax.broadcasted_iota(jnp.int32, (length, length), 0)
        col = lax.broadcasted_iota(jnp.int32, (length, length), 1)
        lower = jnp.where(row >= col, 1.0, 0.0).astype(BF16)
        cum = jnp.zeros((length, heads), F32)
        for part in split_terms(rate, 3)[::-1]:
            cum = cum + jnp.dot(lower, part, preferred_element_type=F32)
        last = cum[length - 1 : length]
        position = lax.broadcasted_iota(jnp.int32, (length, heads), 0).astype(F32)
        start = start_in_block()
        begins = start < length
        carried = jnp.where(begins, 0.0, jnp.exp(last))
        keep = position >= jnp.where(begins, start, 0.0)
        tail = jnp.where(keep, jnp.exp(last - cum), 0.0) * step
        tail_ref[...] = jnp.concatenate(split_terms(tail, 2), axis=1)
        return step, cum, carried, position, start

    for load in loads[:4]:
        load.wait()
    raw = jnp.concatenate(
        [bias_ref[...], decay_ref[...], skip_ref[...], jnp.zeros((5, own_heads), F32)], axis=0
    )
    placed = jnp.zeros((8, heads), F32)
    for part in split_terms(raw, 3):
        placed = placed + jnp.dot(part, place, preferred_element_type=F32)
    loads[6].wait()
    early = decays(placed)[2]
    owner = lax.broadcasted_iota(jnp.int32, (1, heads), 1) // own_heads == zi
    param_ref[...] = jnp.concatenate(
        [placed[0:3], jnp.where(owner, early, 0.0), placed[4:8]], axis=0
    )

    def remote(src, dst, sems, index, device, sent=None):
        return pltpu.make_async_remote_copy(
            src_ref=src, dst_ref=dst, send_sem=sems.at[(0, *index)] if sent is None else sent_sems.at[sent],
            recv_sem=sems.at[(1, *index)] if sent is None else sems.at[index],
            device_id=device, device_id_type=MESH,
        )

    param_copies = [
        remote(param_ref, param_in.at[d], param_sems, (d,), z_peer(d)) for d in range(1, n)
    ]
    decay_copies = [
        remote(decay_out, decay_in.at[d], decay_sems, (d,), z_peer(d)) for d in range(1, n)
    ]
    hop_copies = [
        remote(hop_out, hop_in.at[d], hop_sems, (d,), ctx_peer(d)) for d in range(1, m)
    ]
    row = lax.broadcasted_iota(jnp.int32, (heads, CHUNK), 0)
    lane = lax.broadcasted_iota(jnp.int32, (heads, CHUNK), 1)

    def fill(k, _):
        spread = jnp.where(row == lane // HEAD_DIM + k * chunk_heads, 1.0, 0.0).astype(BF16)
        spread_ref[k, :heads] = spread
        spread_ref[k, heads:] = spread
        return 0

    def turn_keys(g):
        keys_ref[g] = b_ref[:, g * STATE : (g + 1) * STATE].astype(F32).T.astype(BF16)

    bases = (0, count - half)
    soon = {k // per_group for base in bases for k in range(base, base + SKEW)}
    for base in bases:
        lax.fori_loop(base, base + SKEW, fill, 0)
    loads[4].wait()
    for g in sorted(soon):
        turn_keys(g)
    power_ref[...] = jnp.zeros_like(power_ref)
    pl.semaphore_wait(barrier, n - 1 + m - 1)
    for copy in param_copies:
        copy.start()
    for load in loads[-2:]:
        load.start()
    loads[7].wait()

    def settle():
        lax.fori_loop(0, count, fill, 0)
        for g in range(groups):
            if g not in soon:
                turn_keys(g)
        start = start_in_block()
        row = lax.broadcasted_iota(jnp.int32, (length, length), 0).astype(F32)
        col = lax.broadcasted_iota(jnp.int32, (length, length), 1).astype(F32)
        lower = jnp.where(row >= col, 1.0, 0.0)
        same = jnp.where(row >= start, 1.0, 0.0) == jnp.where(col >= start, 1.0, 0.0)
        allowed = jnp.where(same, lower, 0.0)
        loads[5].wait()
        for g in range(groups):
            part = slice(g * STATE, (g + 1) * STATE)
            scores = lax.dot_general(
                c_ref[:, part], b_ref[:, part], (((1,), (1,)), ((), ())), preferred_element_type=F32
            )
            scores_ref[g] = jnp.where(allowed > 0.0, scores, 0.0).astype(BF16)

        for copy in param_copies:
            copy.wait()
        params = param_ref[...]
        for d in range(1, n):
            params = params + param_in[d]
        step, cum, carried, position, start = decays(params)
        decay_out[...] = jnp.broadcast_to(carried, decay_out.shape)
        for copy in decay_copies:
            copy.start()
        middle = cum[length // 2 - 1 : length // 2]
        up_ref[...] = jnp.concatenate(split_terms(jnp.exp(cum - middle), 2), axis=1)
        down_ref[...] = jnp.concatenate(split_terms(jnp.exp(middle - cum) * step, 2), axis=1)
        out_ref[...] = jnp.concatenate(
            split_terms(jnp.where(position < start, jnp.exp(cum), 0.0), 2), axis=1
        )
        rest = jnp.zeros((4, heads), F32)
        widen(jnp.concatenate([carried, carried, params[3:4], params[2:3], rest], axis=0), line_ref)
        loads[8].wait()
        loads[9].wait()

    def step_copy(j, k):
        return remote(step_send.at[j, k], step_recv.at[j, k], step_sems, (j, k), (ctx_partner(j)[0], zi), j)

    def relay_copy(j, k):
        arrived = step_recv.at[j, k]
        return remote(arrived, arrived, relay_sems, (j, k), (ctx_partner(0)[0], zi), bits + j)

    def is_mine(k):
        return lax.rem(k, 2) == lax.rem(ci, 2)

    def send(j, k, value):
        def go():
            sum_ref[k] = value
            step_send[j, k] = value.astype(BF16)
            step_copy(j, k).start()

        if j == bits - 1:
            pl.when(is_last_lower)(go)
        else:
            go()

    def fore_copy(k):
        return remote(fore_send.at[k], fore_recv.at[k], fore_sems, (k,), (ci, lax.rem(zi + 1, n)), 2 * bits)

    def back_copy(k):
        return remote(back_send.at[k], back_recv.at[k], back_sems, (k,), (ci, lax.rem(zi + n - 1, n)), 2 * bits + 1)

    def channels(k):
        return pl.ds(pl.multiple_of(k * CHUNK, CHUNK), CHUNK)

    def states(k):
        return pl.ds(pl.multiple_of((k // per_group) * STATE, STATE), STATE)

    def line(k, slot):
        return line_ref[slot : slot + 1, channels(k)]

    def coef(k, slot):
        return coef_ref[slot : slot + 1, channels(k)]

    is_last_upper = ctx_partner(bits - 1)[1] == 1
    is_last_lower = ctx_partner(bits - 1)[1] == 0

    def write(k):
        weight = jnp.dot(tail_ref[...], spread_ref[k], preferred_element_type=F32)
        scaled = (x_ref[:, channels(k)].astype(F32) * weight).astype(BF16)
        written = jnp.dot(keys_ref[k // per_group], scaled, preferred_element_type=F32)
        own_ref[k] = written
        return written

    def look(*chunks):
        inputs = [x_ref[:, channels(k)].astype(F32) for k in chunks]
        downs = [jnp.dot(down_ref[...], spread_ref[k], preferred_element_type=F32) for k in chunks]
        pulled = [(x * down).astype(BF16) for x, down in zip(inputs, downs)]
        ups = [jnp.dot(up_ref[...], spread_ref[k], preferred_element_type=F32) for k in chunks]
        insides = [
            jnp.dot(scores_ref[k // per_group], p, preferred_element_type=F32)
            for k, p in zip(chunks, pulled)
        ]
        for k, x, up, inside in zip(chunks, inputs, ups, insides):
            inside_ref[k] = up * inside + line(k, 3) * x

    def finish(*pairs):
        frozens = []
        for k, with_back in pairs:
            incoming = before_ref[k]
            if with_back:
                incoming = incoming + back_recv[k].astype(F32)
            frozens.append((fore_recv[k].astype(F32) + line(k, 1) * incoming).astype(BF16))
        for (k, _), frozen in zip(pairs, frozens):
            weight = jnp.dot(out_ref[...], spread_ref[k], preferred_element_type=F32)
            outside = jnp.dot(c_ref[:, states(k)], frozen, preferred_element_type=F32)
            half_gate = 0.5 * gate_ref[:, channels(k)].astype(F32)
            gated = (outside * weight + inside_ref[k]) * (half_gate * (1.0 + jnp.tanh(half_gate)))
            gated_ref[:, channels(k)] = (gated * gain_ref[:, channels(k)]).astype(BF16)
            square = gated * gated
            total = power_ref[...]
            for i in range(CHUNK // 128):
                total = total + square[:, i * 128 : (i + 1) * 128]
            power_ref[...] = total

    fore_at = zi * SKEW
    back_at = (n - 1 - zi) * SKEW
    head_at = jnp.minimum(fore_at, back_at + half)
    rear_at = jnp.minimum(back_at, fore_at + half)

    def iteration(t, _):
        pl.when(t == SKEW)(settle)

        s = t - last_turn

        @pl.when((s >= 0) & (s < both))
        def _():
            finish((second_chunk(s), True), (first_chunk(s), False))

        if second > both:
            @pl.when((s >= both) & (s < second))
            def _():
                finish((second_chunk(s), True))

        if first > both:
            @pl.when((s >= both) & (s < first))
            def _():
                finish((first_chunk(s), False))

        @pl.when(t == TURN)
        def _():
            for copy in decay_copies:
                copy.wait()
            own = decay_out[...]
            before = jnp.ones((8, heads), F32)
            after = jnp.ones((8, heads), F32)
            for d in range(1, n):
                got = decay_in[d]
                before = before * jnp.where(zi >= d, got, 1.0)
                after = after * jnp.where(zi >= d, 1.0, got)
            hop_out[...] = before * own * after
            for copy in hop_copies:
                copy.start()
            skip = param_ref[2:3]
            for d in range(1, n):
                skip = skip + param_in[d, 2:3]
            widen(jnp.concatenate([own[0:1], before[0:1], after[0:1], skip, own[4:8]], axis=0), line_ref)

        @pl.when(t == TURN + hops[0])
        def _():
            for copy in hop_copies:
                copy.wait()
            total = hop_out[...]
            ahead = jnp.ones((8, heads), F32)
            rows = []
            for j in range(bits):
                bit = 1 << j
                is_upper = ctx_partner(j)[1] == 1
                sibling = ctx_partner(j)[0] // bit
                got = jnp.ones((8, heads), F32)
                for d in range(1, m):
                    source = lax.rem(ci + m - d, m)
                    got = got * jnp.where(source // bit == sibling, hop_in[d], 1.0)
                rows.append(jnp.where(is_upper, ahead, 0.0))
                if j < bits - 1:
                    rows.append(jnp.where(is_upper, 1.0, got))
                    rows.append(jnp.where(is_upper, total, 1.0))
                ahead = jnp.where(is_upper, ahead * got, ahead)
                total = total * got
            pad = [jnp.zeros((1, heads), F32)] * (coef_ref.shape[0] - len(rows))
            widen(jnp.concatenate([r[0:1] for r in rows] + pad, axis=0), coef_ref)

        for at, base in ((head_at, 0), (rear_at, count - half)):
            @pl.when((t >= at) & (t < at + half))
            def _(at=at, base=base):
                write(base + t - at)


        def fore(k, is_first):
            @pl.when(zi > 0)
            def _():
                fore_copy(k).wait_recv()

            @pl.when(zi == 0)
            def _():
                fore_recv[k] = jnp.zeros_like(fore_recv[k])
                if is_first:
                    fore_send[k] = own_ref[k].astype(BF16)
                    fore_copy(k).start()

            @pl.when((zi > 0) & (zi < n - 1) if is_first else zi < n - 1)
            def _():
                arrived = fore_recv[k].astype(F32)
                if not is_first:
                    arrived = arrived + line(k, 1) * before_ref[k]
                fore_send[k] = (line(k, 0) * arrived + own_ref[k]).astype(BF16)
                fore_copy(k).start()

        def back(k, is_first):
            @pl.when(zi < n - 1)
            def _():
                back_copy(k).wait_recv()

            @pl.when(zi == n - 1)
            def _():
                back_recv[k] = jnp.zeros_like(back_recv[k])
                if is_first:
                    back_send[k] = own_ref[k].astype(BF16)
                    back_copy(k).start()

            @pl.when((zi > 0) & (zi < n - 1) if is_first else zi > 0)
            def _():
                more = line(k, 2) * own_ref[k] if is_first else before_ref[k]
                back_send[k] = (back_recv[k].astype(F32) + more).astype(BF16)
                back_copy(k).start()

        for at, relay, turned in ((fore_at, fore, 0), (back_at, back, half)):
            s = t - at

            @pl.when((s >= 0) & (s < first))
            def _():
                relay(first_chunk(lax.rem(s + turned, first)), True)

            @pl.when((s >= z_turn) & (s < z_turn + second))
            def _():
                relay(second_chunk(s - z_turn), False)

        def begin(k):
            step_copy(0, k).wait_recv()
            got = step_recv[0, k].astype(F32)
            before_ref[k] = coef(k, 0) * got

            @pl.when(is_mine(k))
            def _():
                send(1, k, sum_ref[k] * coef(k, 1) + coef(k, 2) * got)

        def advance(j, k):
            step_copy(j, k).wait_recv()
            got = step_recv[j, k].astype(F32)

            @pl.when(ctx_partner(j)[1] == 1)
            def _():
                relay_copy(j, k).start()
                before_ref[k] += coef(k, 3 * j) * got

            if j < bits - 1:
                send(j + 1, k, sum_ref[k] * coef(k, 1 + 3 * j) + coef(k, 2 + 3 * j) * got)

        def share(j, k):
            relay_copy(j, k).wait_recv()
            before_ref[k] += coef(k, 3 * j) * step_recv[j, k].astype(F32)

        @pl.when((t >= c_turn) & (t < c_turn + first))
        def _():
            k = first_chunk(t - c_turn)
            value = line(k, 0) * fore_recv[k].astype(F32) + own_ref[k]
            send(0, k, line(k, 2) * value + back_recv[k].astype(F32))

        for begins_at, chunk, length_of, after in (
            (TURN, second_chunk, second, hops), (c_turn, first_chunk, first, fast),
        ):
            for j in range(bits):
                s = t - begins_at - after[j]
                k = chunk(s)
                inside = (s >= 0) & (s < length_of)
                if j == 0:
                    pl.when(inside)(functools.partial(begin, k))
                    continue
                if j == bits - 1:
                    inside = inside & is_last_upper
                pl.when(inside & is_mine(k))(functools.partial(advance, j, k))
                s = s - 1
                k = chunk(s)
                inside = (s >= 0) & (s < length_of) & (ctx_partner(j)[1] == 1)
                pl.when(inside & jnp.logical_not(is_mine(k)))(functools.partial(share, j, k))

        @pl.when((t >= TURN) & (t < TURN + second))
        def _():
            k = second_chunk(t - TURN)
            send(0, k, line(k, 2) * write(k))

        s = t - look_turn

        @pl.when((s >= 0) & (s < both))
        def _():
            look(second_chunk(s), first_chunk(s))

        if first != second:
            rest = second_chunk if second > both else first_chunk

            @pl.when((s >= both) & (s < max(first, second)))
            def _():
                look(rest(s))

        return 0

    steps = last_turn + max(first, second)
    lax.fori_loop(0, steps, iteration, 0)

    def drain(part, sent):
        pltpu.make_async_copy(part, part, sent_sems.at[sent]).wait()

    drain(step_send.at[0], 0)
    for j in range(1, bits):
        is_upper = ctx_partner(j)[1] == 1

        @pl.when(is_upper)
        def _(j=j):
            drain(step_recv.at[j, : count // 2], bits + j)

        if j < bits - 1:
            drain(step_send.at[j, : count // 2], j)
        else:
            @pl.when(jnp.logical_not(is_upper))
            def _(j=j):
                drain(step_send.at[j, : count // 2], j)

    @pl.when(zi < n - 1)
    def _():
        drain(fore_send, 2 * bits)

    @pl.when(zi > 0)
    def _():
        drain(back_send, 2 * bits + 1)


def scale_kernel(gated_ref, power_ref, out_hbm, out_ref, sems):
    length, inner = gated_ref.shape
    tiles = sems.shape[0]
    tile = length // tiles
    width = 1024
    copies = []
    for i in range(tiles):
        rows = slice(i * tile, (i + 1) * tile)
        power = jnp.sum(power_ref[rows], axis=1, keepdims=True)
        factor = lax.rsqrt(power / inner + 1e-05)
        for j in range(inner // width):
            part = slice(j * width, (j + 1) * width)
            out_ref[rows, part] = (gated_ref[rows, part].astype(F32) * factor).astype(BF16)
        copy = pltpu.make_async_copy(out_ref.at[rows], out_hbm.at[rows], sems.at[i])
        copy.start()
        copies.append(copy)
    for copy in copies:
        copy.wait()


def local(
    n, m,
    head_inputs, gate_inputs, write_keys, read_queries, step_logits,
    step_bias, decay_log, skip_scale, norm_gain, document_starts,
):
    length, inner = head_inputs.shape
    heads = step_logits.shape[1]
    groups = write_keys.shape[1] // STATE
    assert length <= BLOCK and BLOCK % length == 0 and m & (m - 1) == 0 and m > 2 and n > 1
    bits = m.bit_length() - 1
    count = inner // CHUNK
    coefs = -(-(3 * bits - 2) // 8) * 8
    assert count % max(n, 4) == 0

    hbm = pl.BlockSpec(memory_space=pltpu.HBM)
    whole = pl.BlockSpec(memory_space=pltpu.VMEM)
    piece = (count, STATE, CHUNK)
    dma = pltpu.SemaphoreType.DMA
    gated, power = pl.pallas_call(
        functools.partial(exchange_kernel, n, m, groups),
        out_shape=(pltpu.VMEM((length, inner), BF16), pltpu.VMEM((length, 128), F32)),
        in_specs=[hbm] * 10,
        out_specs=(whole, whole),
        scratch_shapes=[
            pltpu.VMEM((length, inner), BF16),
            pltpu.VMEM((length, inner), BF16),
            pltpu.VMEM((1, inner), F32),
            pltpu.VMEM(write_keys.shape, BF16),
            pltpu.VMEM(read_queries.shape, BF16),
            pltpu.VMEM(step_logits.shape, BF16),
            pltpu.VMEM((1, step_bias.shape[0]), F32),
            pltpu.VMEM((1, step_bias.shape[0]), F32),
            pltpu.VMEM((1, step_bias.shape[0]), F32),
            pltpu.VMEM((1, document_starts.shape[0]), jnp.int32),
            pltpu.VMEM((groups, STATE, length), BF16),
            pltpu.VMEM((groups, length, length), BF16),
            pltpu.VMEM((count, 2 * heads, CHUNK), BF16),
            pltpu.VMEM((8, heads), F32),
            pltpu.VMEM((length, 2 * heads), BF16),
            pltpu.VMEM((length, 2 * heads), BF16),
            pltpu.VMEM((length, 2 * heads), BF16),
            pltpu.VMEM((length, 2 * heads), BF16),
            pltpu.VMEM((8, inner), F32),
            pltpu.VMEM((coefs, inner), F32),
            pltpu.VMEM(piece, F32),
            pltpu.VMEM(piece, F32),
            pltpu.VMEM(piece, F32),
            pltpu.VMEM((count, length, CHUNK), F32),
            pltpu.VMEM((bits, *piece), BF16),
            pltpu.VMEM((bits, *piece), BF16),
            pltpu.VMEM(piece, BF16),
            pltpu.VMEM(piece, BF16),
            pltpu.VMEM(piece, BF16),
            pltpu.VMEM(piece, BF16),
            pltpu.VMEM((n, 8, heads), F32),
            pltpu.VMEM((8, heads), F32),
            pltpu.VMEM((n, 8, heads), F32),
            pltpu.VMEM((8, heads), F32),
            pltpu.VMEM((m, 8, heads), F32),
            dma((2, n)),
            dma((2, n)),
            dma((2, m)),
            dma((bits, count)),
            dma((bits, count)),
            dma((count,)),
            dma((count,)),
            dma((2 * bits + 2,)),
            dma((10,)),
        ],
        compiler_params=pltpu.CompilerParams(
            collective_id=0, has_side_effects=True, vmem_limit_bytes=58 * 2**20
        ),
        name="exchange",
    )(
        head_inputs, gate_inputs, norm_gain[None], write_keys, read_queries, step_logits,
        step_bias[None], decay_log[None], skip_scale[None], document_starts[None],
    )

    return pl.pallas_call(
        scale_kernel,
        out_shape=jax.ShapeDtypeStruct((length, inner), BF16),
        in_specs=[whole] * 2,
        out_specs=pl.BlockSpec(memory_space=pl.ANY),
        scratch_shapes=[pltpu.VMEM((length, inner), BF16), dma((length // ROWS,))],
        compiler_params=pltpu.CompilerParams(vmem_limit_bytes=20 * 2**20),
        name="scale",
    )(gated, power)


def solution(mesh):
    tokens = P(("ctx", "head"), None)
    return jax.shard_map(
        functools.partial(local, mesh.shape["head"], mesh.shape["ctx"]),
        mesh=mesh,
        in_specs=(tokens,) * 5 + (P("head"), P("head"), P("head"), P(), P("ctx")),
        out_specs=tokens,
        check_vma=False,
    )
```
